32 devices in a mesh: traj: 2 (over x), dom: 16 (over z, y, core).
Axes of the slice: x: 2, y: 2, z: 4, core: 2. Of those that a mesh axis runs over, the one named last changes fastest.
Arguments:
- node_lat: bfloat16 [2, 4096, 512], P('traj', 'dom'), may hold values from -6 to 6
- edge_lat: bfloat16 [2, 8192, 512], P('traj', 'dom'), may hold values from -6 to 6
- grad_edge: bfloat16 [2, 8192, 512], P('traj', 'dom'), may hold values from -6 to 6
- grad_agg: bfloat16 [2, 4096, 512], P('traj', 'dom'), may hold values from -6 to 6
- weight_edge: bfloat16 [512, 512], replicated, may hold values from -0.15625 to 0.15625
- weight_send: bfloat16 [512, 512], replicated, may hold values from -0.15625 to 0.15625
- weight_recv: bfloat16 [512, 512], replicated, may hold values from -0.15625 to 0.15625
- weight_out: bfloat16 [512, 512], replicated, may hold values from -0.25 to 0.25
- edge_src: int32 [8192], P('dom'), may hold values from 0 to 767
- edge_recv_block: int32 [64], P('dom'), may hold values from 0 to 1
- edge_recv_node: int32 [8192], P('dom'), may hold values from 0 to 127
- send_blocks: int32 [64], P('dom'), may hold values from 0 to 1
Outputs:
- agg: bfloat16 [2, 4096, 512], P('traj', 'dom')
- grad_edge_lat: bfloat16 [2, 8192, 512], P('traj', 'dom')
- grad_node_lat: bfloat16 [2, 4096, 512], P('traj', 'dom')
- weight_grads: float32 [4, 512, 512], P(None, 'dom')
The draws below stay inside these ranges and needn't reach their ends.
Inputs may be any that keep to these rules, and one draw needn't show every extreme that they name: edge_src // 128 is a slot below 6.
All inputs are finite; a program needn't handle non-finite values.
Results may differ from the reference program's by a relative error of at most 0.012.
Values may be sent and summed in bfloat16 or wider, within the bound.
No kernel may reach another device: no remote copies, remote signals or barrier semaphores. Data moves between devices by JAX's collectives and lax.ppermute only.
A program may use at most 64 MiB of HBM per device.

```python
import jax
import jax.numpy as jnp
from jax import lax

D = 512
EB_DEV = 4
NB_DEV = 2
ROUNDS = 4
EDGES = 8192
NODES = 4096
EDGE_BLOCKS = 64
SEND_ROWS = 64
N_TRAJ = 2
N_DOM = 16


def plant(array, stream_key, low, high):
    longest = array.shape.index(max(array.shape))
    spots = []
    for shift in (0, 1):
        where = [jax.random.randint(jax.random.fold_in(stream_key, axis), (), 0, length) for axis, length in enumerate(array.shape)]
        where[longest] = (where[longest] + shift) % array.shape[longest]
        spots.append(tuple(where))
    return array.at[spots[0]].set(low).at[spots[1]].set(high)


def steps_of(rng, dims, cuts, low, high):
    def one(axis_at, shards_of):
        heights = jax.random.uniform(jax.random.fold_in(jax.random.fold_in(rng, 6), axis_at), (shards_of,), jnp.float32, low / len(cuts), high / len(cuts))
        return jnp.repeat(jnp.exp(heights), dims[axis_at] // shards_of).reshape((-1,) + (1,) * (len(dims) - axis_at - 1))

    loudness = one(*cuts[0])
    for cut in cuts[1:]:
        loudness = loudness * one(*cut)
    return loudness


def normal_values(stream_key, shape, width, limit, cuts=(), kind=jnp.bfloat16):
    gain = steps_of(stream_key, shape, cuts, -0.22, 0.18) if cuts else 1.0
    array = jax.random.normal(stream_key, shape, jnp.float32) * width * gain
    return jnp.minimum(jnp.maximum(array, -limit), limit).astype(kind)


def setup_inputs(seed: int = 0) -> dict:
    streams_of = jax.random.split(jax.random.key(seed), 13)
    node_lat = normal_values(streams_of[0], (N_TRAJ, NODES, D), 1.0, 6.0, ((0, 2), (1, 16)))
    edge_lat = normal_values(streams_of[1], (N_TRAJ, EDGES, D), 1.0, 6.0, ((0, 2), (1, 16)))
    grad_edge = normal_values(streams_of[2], (N_TRAJ, EDGES, D), 1.0, 6.0, ((0, 2), (1, 16)))
    grad_agg = normal_values(streams_of[3], (N_TRAJ, NODES, D), 1.0, 6.0, ((0, 2), (1, 16)))
    weight_edge = normal_values(streams_of[4], (D, D), (3 * D) ** -0.5, 0.15625)
    weight_send = normal_values(streams_of[5], (D, D), (3 * D) ** -0.5, 0.15625)
    weight_recv = normal_values(streams_of[6], (D, D), (3 * D) ** -0.5, 0.15625)
    weight_out = normal_values(streams_of[7], (D, D), D ** -0.5, 0.25)
    edge_src = plant(jax.random.randint(streams_of[8], (EDGES,), 0, (NB_DEV + ROUNDS) * 128), jax.random.fold_in(streams_of[8], 1), 0, ((NB_DEV + ROUNDS) * 128) - 1).astype(jnp.int32)
    edge_recv_block = plant(jax.random.randint(streams_of[9], (EDGE_BLOCKS,), 0, NB_DEV), jax.random.fold_in(streams_of[9], 1), 0, NB_DEV - 1).astype(jnp.int32)
    edge_recv_node = plant(jax.random.randint(streams_of[10], (EDGES,), 0, 128), jax.random.fold_in(streams_of[10], 1), 0, 127).astype(jnp.int32)
    send_blocks = plant(jax.random.randint(streams_of[11], (SEND_ROWS,), 0, NB_DEV), jax.random.fold_in(streams_of[11], 1), 0, NB_DEV - 1).astype(jnp.int32)
    return {"node_lat": node_lat, "edge_lat": edge_lat, "grad_edge": grad_edge, "grad_agg": grad_agg, "weight_edge": weight_edge, "weight_send": weight_send, "weight_recv": weight_recv, "weight_out": weight_out, "edge_src": edge_src, "edge_recv_block": edge_recv_block, "edge_recv_node": edge_recv_node, "send_blocks": send_blocks}


def dot_rows(former, latter):
    return lax.dot_general(former, latter, (((0,), (0,)), ((), ())), preferred_element_type=jnp.float32)

def dot_cols(former, latter):
    return lax.dot_general(former, latter, (((1,), (1,)), ((), ())), preferred_element_type=jnp.float32)

def silu_grad(preact):
    sigmoid_val = jax.nn.sigmoid(preact)
    return sigmoid_val * (1.0 + preact * (1.0 - sigmoid_val))

def indices(edge_src, edge_recv_block, edge_recv_node, send_blocks):
    devices = jnp.arange(N_DOM, dtype=jnp.int32)
    sent_blocks = send_blocks.reshape(N_DOM, ROUNDS)
    columns = [devices[:, None] * NB_DEV + jnp.arange(NB_DEV, dtype=jnp.int32)[None, :]]
    for section in range(ROUNDS):
        partner = jnp.bitwise_xor(devices, 1 << section)
        columns.append((partner * NB_DEV + sent_blocks[partner, section])[:, None])
    slot_table = jnp.concatenate(columns, axis=1).astype(jnp.int32)
    edge_owner = (jnp.arange(EDGES, dtype=jnp.int32) // (EB_DEV * 128)).astype(jnp.int32)
    sender = slot_table[edge_owner, edge_src // 128] * 128 + edge_src % 128
    block_ids = jnp.repeat(edge_recv_block, 128, total_repeat_length=EDGES)
    receiver = edge_owner * (NB_DEV * 128) + block_ids * 128 + edge_recv_node
    return (sender.astype(jnp.int32), receiver.astype(jnp.int32))

def reference(node_lat, edge_lat, grad_edge, grad_agg, weight_edge, weight_send, weight_recv, weight_out, edge_src, edge_recv_block, edge_recv_node, send_blocks):
    sender, receiver = indices(edge_src, edge_recv_block, edge_recv_node, send_blocks)
    weight_sum = jnp.zeros((4, D, D), jnp.float32)
    agg_list, edge_list, node_list = ([], [], [])
    for member in range(N_TRAJ):
        node_rows = node_lat[member]
        edge_rows = edge_lat[member]
        send_rows = node_rows[sender]
        recv_rows = node_rows[receiver]
        preact = jnp.dot(edge_rows, weight_edge, preferred_element_type=jnp.float32)
        preact = preact + jnp.dot(send_rows, weight_send, preferred_element_type=jnp.float32)
        preact = preact + jnp.dot(recv_rows, weight_recv, preferred_element_type=jnp.float32)
        hidden = jax.nn.silu(preact).astype(jnp.bfloat16)
        projected = jnp.dot(hidden, weight_out, preferred_element_type=jnp.float32)
        centered = projected - lax.optimization_barrier(jnp.mean(projected, axis=1, keepdims=True))
        inv_std = lax.rsqrt(lax.optimization_barrier(jnp.mean(centered * centered, axis=1, keepdims=True)) + 1e-05)
        normed = centered * inv_std
        message = normed.astype(jnp.bfloat16)
        agg = jax.ops.segment_sum(message.astype(jnp.float32), receiver, num_segments=NODES)
        grad_msg = grad_edge[member].astype(jnp.float32) + grad_agg[member][receiver].astype(jnp.float32)
        grad_proj = inv_std * (grad_msg - lax.optimization_barrier(jnp.mean(grad_msg, axis=1, keepdims=True)) - normed * lax.optimization_barrier(jnp.mean(grad_msg * normed, axis=1, keepdims=True)))
        grad_proj = grad_proj.astype(jnp.bfloat16)
        grad_preact = (dot_cols(grad_proj, weight_out) * silu_grad(preact)).astype(jnp.bfloat16)
        weight_sum = weight_sum + jnp.stack([dot_rows(edge_rows, grad_preact), dot_rows(send_rows, grad_preact), dot_rows(recv_rows, grad_preact), dot_rows(hidden, grad_proj)])
        grad_edges = grad_edge[member].astype(jnp.float32) + dot_cols(grad_preact, weight_edge)
        grad_nodes = jax.ops.segment_sum(dot_cols(grad_preact, weight_send), sender, num_segments=NODES)
        grad_nodes = grad_nodes + jax.ops.segment_sum(dot_cols(grad_preact, weight_recv), receiver, num_segments=NODES)
        agg_list.append(agg.astype(jnp.bfloat16))
        edge_list.append(grad_edges.astype(jnp.bfloat16))
        node_list.append(grad_nodes.astype(jnp.bfloat16))
    return (jnp.stack(agg_list), jnp.stack(edge_list), jnp.stack(node_list), weight_sum)
```

```python
import functools

import jax
import jax.numpy as jnp
from jax import lax
from jax.experimental import pallas as pl
from jax.experimental.pallas import tpu as pltpu
from jax.sharding import Mesh, PartitionSpec as P

LANES = 128
BF16 = jnp.bfloat16
F32 = jnp.float32
VMEM = pl.BlockSpec(memory_space=pltpu.VMEM)
SMEM = pl.BlockSpec(memory_space=pltpu.SMEM)


def dot(former, latter):
    return jnp.dot(former, latter, preferred_element_type=F32)


def dot_rows(former, latter):
    return lax.dot_general(former, latter, (((0,), (0,)), ((), ())), preferred_element_type=F32)


def dot_cols(former, latter):
    return lax.dot_general(former, latter, (((1,), (1,)), ((), ())), preferred_element_type=F32)


def call(body, outs, ins, name):
    return pl.pallas_call(
        body,
        out_shape=[jax.ShapeDtypeStruct(shape, kind) for shape, kind in outs],
        in_specs=ins,
        out_specs=[VMEM] * len(outs),
        name=name,
    )


def swap(array, axis):
    return lax.ppermute(array, axis, [(0, 1), (1, 0)])


def down_rows(row, count):
    return jnp.transpose(jnp.broadcast_to(row, (LANES, count)))


def onehot_cols(index_cols, first, blocks):
    lane = lax.broadcasted_iota(jnp.int32, index_cols.shape, 1)
    parts = [
        jnp.where(index_cols == lane + (first + LANES * block), 1.0, 0.0).astype(BF16)
        for block in range(blocks)
    ]
    return jnp.concatenate(parts, axis=1)


def onehot_rows(index_row, first, rows):
    node = lax.broadcasted_iota(jnp.int32, (rows, index_row.shape[1]), 0) + first
    return jnp.where(node == index_row, 1.0, 0.0).astype(BF16)


def receiver_row(recv_block, recv_node):
    edges = recv_node.shape[1]
    return jnp.concatenate(
        [
            recv_node[:, LANES * block : LANES * (block + 1)] + recv_block[block] * LANES
            for block in range(edges // LANES)
        ],
        axis=1,
    )


def pick_body(send_blocks, node_lat, *lent):
    for section, out in enumerate(lent):
        out[...] = node_lat[pl.ds(pl.multiple_of(send_blocks[section] * LANES, LANES), LANES), :]


def early_body(
    recv_block, edge_src, recv_node, node_lat, edge_lat, grad_edge, grad_agg, weight_edge,
    weight_recv, recv_out, send_out, preact_out, grad_msg_out,
):
    nodes = node_lat.shape[0]
    edges = edge_lat.shape[0]
    receiver = down_rows(receiver_row(recv_block, recv_node[...]), edges)
    sender = down_rows(edge_src[...], edges)
    hot_recv = onehot_cols(receiver, 0, nodes // LANES)
    recv_rows = dot(hot_recv, node_lat[...]).astype(BF16)
    recv_out[...] = recv_rows
    send_out[...] = dot(onehot_cols(sender, 0, nodes // LANES), node_lat[...]).astype(BF16)
    preact_out[...] = dot(edge_lat[...], weight_edge[...]) + dot(recv_rows, weight_recv[...])
    grad_msg_out[...] = grad_edge[...].astype(F32) + dot(hot_recv, grad_agg[...])


def main_body(
    rounds, parts, core, recv_block, edge_src, recv_node, recv_rows, send_own, preact_own,
    grad_msg, edge_lat, weight_send, weight_out, *refs,
):
    borrowed = refs[:rounds]
    (give_out, keep_out, grad_preact_out, message_out, own_out, recv_out) = refs[rounds : rounds + 6]
    back_out = refs[rounds + 6 : 2 * rounds + 6]
    table, sums, send_ref, hidden_ref, grad_proj_ref = refs[2 * rounds + 6 :]
    edges, features = edge_lat.shape
    nodes = own_out.shape[0]
    for section in range(rounds):
        table[LANES * section : LANES * (section + 1), :] = borrowed[section][...]
    sender = down_rows(edge_src[...], edges)
    step = edges // 2
    for start in range(0, edges, step):
        rows = slice(start, start + step)
        hot = onehot_cols(sender[rows], nodes, rounds)
        send = (send_own[rows, :].astype(F32) + dot(hot, table[...])).astype(BF16)
        send_ref[rows, :] = send
        preact = preact_own[rows, :] + dot(send, weight_send[...])
        sigmoid = jax.nn.sigmoid(preact)
        hidden = (preact * sigmoid).astype(BF16)
        hidden_ref[rows, :] = hidden
        slope = sigmoid * (1.0 + preact * (1.0 - sigmoid))
        projected = dot(hidden, weight_out[...])
        centered = projected - jnp.mean(projected, axis=1, keepdims=True)
        inv_std = lax.rsqrt(jnp.mean(centered * centered, axis=1, keepdims=True) + 1e-05)
        normed = centered * inv_std
        message_out[rows, :] = normed.astype(BF16)
        grad = grad_msg[rows, :]
        grad_proj = inv_std * (
            grad
            - jnp.mean(grad, axis=1, keepdims=True)
            - normed * jnp.mean(grad * normed, axis=1, keepdims=True)
        )
        grad_proj = grad_proj.astype(BF16)
        grad_proj_ref[rows, :] = grad_proj
        grad_preact_out[rows, :] = (dot_cols(grad_proj, weight_out[...]) * slope).astype(BF16)
    grad_preact = grad_preact_out[...]
    receiver = receiver_row(recv_block, recv_node[...])
    slot_sums = dot(onehot_rows(edge_src[...], 0, nodes + rounds * LANES), grad_preact)
    own_out[...] = slot_sums[:nodes]
    for section in range(rounds):
        first = nodes + LANES * section
        back_out[section][...] = slot_sums[first : first + LANES].astype(BF16)
    recv_out[...] = dot(onehot_rows(receiver, 0, nodes), grad_preact)
    sums[3] = dot_rows(hidden_ref[...], grad_proj_ref[...])
    sums[0] = dot_rows(edge_lat[...], grad_preact)
    sums[1] = dot_rows(send_ref[...], grad_preact)
    sums[2] = dot_rows(recv_rows[...], grad_preact)
    members, mids, tops, take = parts
    share = features // (2 * mids * tops)
    per_part = sums.shape[0] // members
    for target, flip in ((keep_out, 0), (give_out, 1)):
        side = core[0] ^ flip
        for part in range(members):
            for mid in range(mids):
                for top in range(tops):
                    first = pl.multiple_of(((top * mids + mid) * 2 + side) * share, share)
                    piece = [
                        sums[part * per_part + which, pl.ds(first, share), :]
                        for which in range(per_part)
                    ]
                    place = ((part * mids + mid) * tops + top) * take
                    target[place : place + take, :] = jnp.concatenate(piece, axis=0).astype(
                        target.dtype
                    )


def add_body(keep, got, out):
    out[...] = (keep[...] + got[...].astype(F32)).astype(BF16)


def fold_body(groups, take, top, got, keep_out, give_out):
    for target, flip in ((keep_out, 0), (give_out, 1)):
        side = top[0] ^ flip
        total = None
        for group in range(groups):
            first = pl.multiple_of((2 * group + side) * take, take)
            piece = got[pl.ds(first, take), :].astype(F32)
            total = piece if total is None else total + piece
        target[...] = total.astype(target.dtype)


def edge_body(recv_block, recv_node, grad_preact, message, grad_edge, weight_edge, agg_out, edge_out):
    receiver = receiver_row(recv_block, recv_node[...])
    agg_out[...] = dot(onehot_rows(receiver, 0, agg_out.shape[0]), message[...]).astype(BF16)
    edge_out[...] = (
        grad_edge[...].astype(F32) + dot_cols(grad_preact[...], weight_edge[...])
    ).astype(BF16)


def dot_cols_split(former, latter):
    high = former.astype(BF16)
    low = (former - high.astype(F32)).astype(BF16)
    return dot_cols(high, latter) + dot_cols(low, latter)


def node_body(send_blocks, own_sums, recv_sums, weight_send, weight_recv, *refs):
    returned, out, total = refs[:-2], refs[-2], refs[-1]
    total[...] = own_sums[...]
    for section, block in enumerate(returned):
        rows = pl.ds(pl.multiple_of(send_blocks[section] * LANES, LANES), LANES)
        total[rows, :] = total[rows, :] + block[...].astype(F32)
    out[...] = (
        dot_cols_split(total[...], weight_send[...])
        + dot_cols_split(recv_sums[...], weight_recv[...])
    ).astype(BF16)


def per_device(
    traj_axes, dom_axes, node_lat, edge_lat, grad_edge, grad_agg, weight_edge, weight_send,
    weight_recv, weight_out, edge_src, edge_recv_block, edge_recv_node, send_blocks,
):
    node_lat, edge_lat, grad_edge, grad_agg = node_lat[0], edge_lat[0], grad_edge[0], grad_agg[0]
    nodes, features = node_lat.shape
    edges = edge_lat.shape[0]
    rounds = send_blocks.shape[0]
    edge_src = edge_src.reshape(1, edges)
    recv_node = edge_recv_node.reshape(1, edges)
    bits = dom_axes[::-1]
    domains = 2 ** len(bits)
    share = 4 * features // domains
    split = traj_axes[:1] if share >= 32 else ()
    take = share >> len(split)
    mids = bits[1:-1][::-1]
    members = 2 ** len(split)
    groups = 2 ** (len(mids) + len(split))
    half = 2 * features

    lent = call(
        pick_body, [((LANES, features), BF16)] * rounds, [SMEM, VMEM], "pick"
    )(send_blocks, node_lat)
    borrowed = [None] * rounds
    for section in reversed(range(rounds)):
        borrowed[section] = swap(lent[section], bits[section])

    recv_rows, send_own, preact_own, grad_msg = call(
        early_body,
        [((edges, features), BF16)] * 2 + [((edges, features), F32)] * 2,
        [SMEM] + [VMEM] * 8,
        "early",
    )(edge_recv_block, edge_src, recv_node, node_lat, edge_lat, grad_edge, grad_agg, weight_edge, weight_recv)

    core = lax.axis_index(bits[0]).astype(jnp.int32).reshape(1)
    main = pl.pallas_call(
        functools.partial(main_body, rounds, (members, 2 ** len(mids), 2, take)),
        out_shape=[
            jax.ShapeDtypeStruct((half, features), BF16),
            jax.ShapeDtypeStruct((half, features), F32),
            jax.ShapeDtypeStruct((edges, features), BF16),
            jax.ShapeDtypeStruct((edges, features), BF16),
            jax.ShapeDtypeStruct((nodes, features), F32),
            jax.ShapeDtypeStruct((nodes, features), F32),
        ]
        + [jax.ShapeDtypeStruct((LANES, features), BF16)] * rounds,
        in_specs=[SMEM, SMEM] + [VMEM] * (9 + rounds),
        out_specs=[VMEM] * (6 + rounds),
        scratch_shapes=[
            pltpu.VMEM((rounds * LANES, features), BF16),
            pltpu.VMEM((4, features, features), F32),
            pltpu.VMEM((edges, features), BF16),
            pltpu.VMEM((edges, features), BF16),
            pltpu.VMEM((edges, features), BF16),
        ],
        name="main",
    )
    give, keep, grad_preact, message, own_sums, recv_sums, *back = main(
        core, edge_recv_block, edge_src, recv_node, recv_rows, send_own, preact_own, grad_msg,
        edge_lat, weight_send, weight_out, *borrowed,
    )

    got = swap(give, bits[0])
    returned = [None] * rounds
    for section in reversed(range(rounds)):
        returned[section] = swap(back[section], bits[section])

    chip = call(add_body, [((half, features), BF16)], [VMEM, VMEM], "chip")(keep, got)[0]
    spread = lax.all_to_all(chip, split + mids, split_axis=0, concat_axis=0, tiled=True)
    agg, grad_edges = call(
        edge_body,
        [((nodes, features), BF16), ((edges, features), BF16)],
        [SMEM] + [VMEM] * 5,
        "edge",
    )(edge_recv_block, recv_node, grad_preact, message, grad_edge, weight_edge)
    grad_nodes = pl.pallas_call(
        node_body,
        out_shape=jax.ShapeDtypeStruct((nodes, features), BF16),
        in_specs=[SMEM] + [VMEM] * (4 + rounds),
        out_specs=VMEM,
        scratch_shapes=[pltpu.VMEM((nodes, features), F32)],
        name="node",
    )(send_blocks, own_sums, recv_sums, weight_send, weight_recv, *returned)

    top = lax.axis_index(bits[-1]).astype(jnp.int32).reshape(1)
    keep_top, give_top = call(
        functools.partial(fold_body, groups, take),
        [((take, features), F32), ((take, features), BF16)],
        [SMEM, VMEM],
        "fold",
    )(top, spread)
    total = keep_top + swap(give_top, bits[-1]).astype(F32)
    for axis in traj_axes[len(split) :]:
        sent = total.astype(BF16)
        total = sent.astype(F32) + swap(sent, axis).astype(F32)
    total = total.astype(BF16)
    if split:
        other = swap(total, split[0])
        first = lax.axis_index(split[0]) == 0
        total = jnp.concatenate(
            [jnp.where(first, total, other), jnp.where(first, other, total)], axis=0
        )
    weight_grads = total.astype(F32).reshape(4, share // 4, features)
    return agg[None], grad_edges[None], grad_nodes[None], weight_grads


def solution(mesh):
    traj_axes = tuple(f"t{bit}" for bit in reversed(range(mesh.shape["traj"].bit_length() - 1)))
    dom_axes = tuple(f"d{bit}" for bit in reversed(range(mesh.shape["dom"].bit_length() - 1)))
    names = traj_axes + dom_axes
    bit_mesh = Mesh(mesh.devices.reshape((2,) * len(names)), names)
    rows = P(traj_axes, dom_axes, None)
    in_specs = (rows,) * 4 + (P(),) * 4 + (P(dom_axes),) * 4
    out_specs = (rows,) * 3 + (P(None, dom_axes, None),)
    return jax.shard_map(
        functools.partial(per_device, traj_axes, dom_axes),
        mesh=bit_mesh,
        in_specs=in_specs,
        out_specs=out_specs,
        check_vma=False,
    )
```

```python
import functools

import jax
import jax.numpy as jnp
from jax import lax
from jax.experimental import pallas as pl
from jax.experimental.pallas import tpu as pltpu
from jax.sharding import Mesh, PartitionSpec as P


LANES = 128
ROOM = 24 << 20
BF16 = jnp.bfloat16
F32 = jnp.float32
VMEM = pl.BlockSpec(memory_space=pltpu.VMEM)
SMEM = pl.BlockSpec(memory_space=pltpu.SMEM)


def dot(former, latter):
    return jnp.dot(former, latter, preferred_element_type=F32)


def dot_rows(former, latter):
    return lax.dot_general(former, latter, (((0,), (0,)), ((), ())), preferred_element_type=F32)


def dot_cols(former, latter):
    return lax.dot_general(former, latter, (((1,), (1,)), ((), ())), preferred_element_type=F32)


def near(array):
    return pltpu.with_memory_space_constraint(array, pltpu.VMEM)


def far(array):
    return pltpu.with_memory_space_constraint(array, pltpu.HBM)


def call(body, outs, ins, kept=True, scratch=()):
    fresh = pltpu.VMEM if kept else jax.ShapeDtypeStruct
    return pl.pallas_call(
        body,
        out_shape=[fresh(shape, kind) for shape, kind in outs],
        in_specs=ins,
        out_specs=[VMEM] * len(outs),
        scratch_shapes=scratch,
        compiler_params=pltpu.CompilerParams(vmem_limit_bytes=ROOM),
    )


def swap(array, axis):
    return lax.ppermute(array, axis, [(0, 1), (1, 0)])


def down_rows(row, count):
    return jnp.transpose(jnp.broadcast_to(row, (LANES, count)))


def onehot_cols(index_cols, first, blocks):
    lane = lax.broadcasted_iota(jnp.int32, index_cols.shape, 1)
    parts = [
        jnp.where(index_cols == lane + (first + LANES * block), 1.0, 0.0).astype(BF16)
        for block in range(blocks)
    ]
    return jnp.concatenate(parts, axis=1)


def onehot_rows(index_row, first, rows):
    node = lax.broadcasted_iota(jnp.int32, (rows, index_row.shape[1]), 0) + first
    return jnp.where(node == index_row, 1.0, 0.0).astype(BF16)


def receiver_row(recv_block, recv_node):
    edges = recv_node.shape[1]
    return jnp.concatenate(
        [
            recv_node[:, LANES * block : LANES * (block + 1)] + recv_block[block] * LANES
            for block in range(edges // LANES)
        ],
        axis=1,
    )


def pick_body(send_blocks, node_lat, *lent):
    for section, out in enumerate(lent):
        out[...] = node_lat[pl.ds(pl.multiple_of(send_blocks[section] * LANES, LANES), LANES), :]


def early_body(
    rounds, recv_block, edge_src, recv_node, node_lat, edge_lat, grad_edge, grad_agg, weight_edge,
    weight_recv, recv_out, send_out, hot_out, preact_out, grad_msg_out,
):
    nodes = node_lat.shape[0]
    edges = edge_lat.shape[0]
    receiver = down_rows(receiver_row(recv_block, recv_node[...]), edges)
    sender = down_rows(edge_src[...], edges)
    hot_recv = onehot_cols(receiver, 0, nodes // LANES)
    recv_rows = dot(hot_recv, node_lat[...]).astype(BF16)
    recv_out[...] = recv_rows
    send_out[...] = dot(onehot_cols(sender, 0, nodes // LANES), node_lat[...]).astype(BF16)
    hot_out[...] = onehot_cols(sender, nodes, rounds)
    preact_out[...] = dot(edge_lat[...], weight_edge[...]) + dot(recv_rows, weight_recv[...])
    grad_msg_out[...] = grad_edge[...].astype(F32) + dot(hot_recv, grad_agg[...])


def main_body(
    rounds, plan, place, recv_rows, send_own, hot, preact_own, grad_msg, edge_lat, weight_send,
    weight_out, *refs,
):
    borrowed = refs[:rounds]
    give_out, keep_out, grad_preact_out, message_out = refs[rounds : rounds + 4]
    table, sums, send_ref, hidden_ref, grad_proj_ref = refs[rounds + 4 :]
    edges = edge_lat.shape[0]
    for section in range(rounds):
        table[LANES * section : LANES * (section + 1), :] = borrowed[section][...]
    step = edges // 2
    for start in range(0, edges, step):
        rows = slice(start, start + step)
        send = (send_own[rows, :].astype(F32) + dot(hot[rows, :], table[...])).astype(BF16)
        send_ref[rows, :] = send
        preact = preact_own[rows, :] + dot(send, weight_send[...])
        sigmoid = jax.nn.sigmoid(preact)
        hidden = (preact * sigmoid).astype(BF16)
        hidden_ref[rows, :] = hidden
        slope = sigmoid * (1.0 + preact * (1.0 - sigmoid))
        projected = dot(hidden, weight_out[...])
        centered = projected - jnp.mean(projected, axis=1, keepdims=True)
        inv_std = lax.rsqrt(jnp.mean(centered * centered, axis=1, keepdims=True) + 1e-05)
        normed = centered * inv_std
        message_out[rows, :] = normed.astype(BF16)
        grad = grad_msg[rows, :]
        grad_proj = inv_std * (
            grad
            - jnp.mean(grad, axis=1, keepdims=True)
            - normed * jnp.mean(grad * normed, axis=1, keepdims=True)
        )
        grad_proj = grad_proj.astype(BF16)
        grad_proj_ref[rows, :] = grad_proj
        grad_preact_out[rows, :] = (dot_cols(grad_proj, weight_out[...]) * slope).astype(BF16)
    grad_preact = grad_preact_out[...]
    sums[3] = dot_rows(hidden_ref[...], grad_proj_ref[...])
    sums[0] = dot_rows(edge_lat[...], grad_preact)
    sums[1] = dot_rows(send_ref[...], grad_preact)
    sums[2] = dot_rows(recv_rows[...], grad_preact)
    pieces, share = plan
    at = 0
    for whiches, flip, domain in pieces:
        for target, side in ((keep_out, 0), (give_out, 1)):
            first = pl.multiple_of((place[1] ^ (domain | side)) * share, share)
            parts = [
                sums[which ^ (flip * place[0]), pl.ds(first, share), :] for which in whiches
            ]
            count = share * len(parts)
            block = parts[0] if len(parts) == 1 else jnp.concatenate(parts, axis=0)
            target[at : at + count, :] = block.astype(target.dtype)
        at += count


def sums_body(recv_block, edge_src, recv_node, grad_preact, own_out, recv_out, *back_out):
    nodes = own_out.shape[0]
    rounds = len(back_out)
    receiver = receiver_row(recv_block, recv_node[...])
    rows = grad_preact[...]
    slot_sums = dot(onehot_rows(edge_src[...], 0, nodes + rounds * LANES), rows)
    own_out[...] = slot_sums[:nodes]
    for section in range(rounds):
        first = nodes + LANES * section
        back_out[section][...] = slot_sums[first : first + LANES].astype(BF16)
    recv_out[...] = dot(onehot_rows(receiver, 0, nodes), rows)


def split_body(colours, keep, got, *outs):
    span = keep.shape[0] // colours
    for colour in range(colours):
        keep_out, give_out = outs[2 * colour : 2 * colour + 2]
        for target, first in ((keep_out, span * colour), (give_out, span * colour + span // 2)):
            rows = slice(first, first + span // 2)
            target[...] = (keep[rows, :] + got[rows, :].astype(F32)).astype(target.dtype)


def merge_body(colours, size, *refs):
    keep_out, give_out = refs[2 * colours :]
    runs = refs[0].shape[0] // size
    for colour in range(colours):
        keep, got = refs[2 * colour : 2 * colour + 2]
        for run in range(runs):
            target = keep_out if run < runs // 2 else give_out
            rows = slice(run * size, (run + 1) * size)
            at = ((run % (runs // 2)) * colours + colour) * size
            target[at : at + size, :] = (keep[rows, :] + got[rows, :].astype(F32)).astype(
                target.dtype
            )


def round_body(keep, got, out):
    out[...] = (keep[...] + got[...].astype(F32)).astype(BF16)


def finish_body(place, *refs):
    *parts, out = refs
    take = parts[0].shape[0]
    for flip, part in enumerate(parts):
        first = pl.multiple_of((place[0] ^ flip) * take, take)
        out[pl.ds(first, take), :] = part[...].astype(F32)


def edge_body(recv_block, recv_node, grad_preact, message, grad_edge, weight_edge, agg_out, edge_out):
    receiver = receiver_row(recv_block, recv_node[...])
    agg_out[...] = dot(onehot_rows(receiver, 0, agg_out.shape[0]), message[...]).astype(BF16)
    edge_out[...] = (
        grad_edge[...].astype(F32) + dot_cols(grad_preact[...], weight_edge[...])
    ).astype(BF16)


def dot_cols_split(former, latter):
    high = former.astype(BF16)
    low = (former - high.astype(F32)).astype(BF16)
    return dot_cols(high, latter) + dot_cols(low, latter)


def node_body(send_blocks, own_sums, recv_sums, weight_send, weight_recv, *refs):
    returned, out, total = refs[:-2], refs[-2], refs[-1]
    total[...] = own_sums[...]
    for section, block in enumerate(returned):
        rows = pl.ds(pl.multiple_of(send_blocks[section] * LANES, LANES), LANES)
        total[rows, :] = total[rows, :] + block[...].astype(F32)
    out[...] = (
        dot_cols_split(total[...], weight_send[...])
        + dot_cols_split(recv_sums[...], weight_recv[...])
    ).astype(BF16)


def layout(share, parts, tops):
    colours = 2 if parts == 2 and tops and share >= 16 else 1
    per_part = 4 // parts
    orders = [(["part"] if parts == 2 else []) + list(range(1, tops + 1))]
    if colours == 2:
        orders.append([1, "part"] + list(range(2, tops + 1)))
    pieces = []
    for colour, order in enumerate(orders):
        whiches = tuple(range(per_part))[colour * per_part // colours :][: per_part // colours]
        for index in range(2 ** len(order)):
            domain, flip = 0, 0
            for level, bit in enumerate(order):
                on = index >> (len(order) - 1 - level) & 1
                if bit == "part":
                    flip = on
                else:
                    domain |= on << bit
            pieces.append((tuple(which ^ (flip * per_part) for which in whiches), per_part, domain))
    return tuple(pieces), orders, share * per_part // colours


def per_device(
    traj_axes, dom_axes, node_lat, edge_lat, grad_edge, grad_agg, weight_edge, weight_send,
    weight_recv, weight_out, edge_src, edge_recv_block, edge_recv_node, send_blocks,
):
    node_lat, edge_lat, grad_edge, grad_agg = node_lat[0], edge_lat[0], grad_edge[0], grad_agg[0]
    nodes, features = node_lat.shape
    edges = edge_lat.shape[0]
    rounds = send_blocks.shape[0]
    edge_src = edge_src.reshape(1, edges)
    recv_node = edge_recv_node.reshape(1, edges)
    bits = dom_axes[::-1]
    share = features // 2 ** len(bits)
    split = traj_axes[:1] if 2 * share >= 16 else ()
    pieces, orders, size = layout(share, 1 + len(split), len(bits) - 1)
    colours = len(orders)
    half = 2 * features
    wide = ((edges, features), BF16)
    wide_sum = ((edges, features), F32)
    node_sum = ((nodes, features), F32)
    block = ((LANES, features), BF16)
    part = lax.axis_index(split[0]) if split else 0
    place = jnp.stack([jnp.int32(part), lax.axis_index(dom_axes).astype(jnp.int32)])

    lent = call(pick_body, [block] * rounds, [SMEM, VMEM])(
        far(send_blocks), far(node_lat)
    )
    borrowed = [swap(lent[section], bits[section]) for section in range(rounds)]
    recv_rows, send_own, hot, preact_own, grad_msg = call(
        functools.partial(early_body, rounds),
        [wide, wide, ((edges, rounds * LANES), BF16), wide_sum, wide_sum],
        [SMEM] + [VMEM] * 8,
    )(
        *map(far, (edge_recv_block, edge_src, recv_node, node_lat, edge_lat)),
        *map(far, (grad_edge, grad_agg, weight_edge, weight_recv)),
    )
    give, keep, grad_preact, message = call(
        functools.partial(main_body, rounds, (pieces, share)),
        [((half, features), BF16), ((half, features), F32), wide, wide],
        [SMEM] + [VMEM] * (8 + rounds),
        scratch=[
            pltpu.VMEM((rounds * LANES, features), BF16),
            pltpu.VMEM((4, features, features), F32),
            pltpu.VMEM((edges, features), BF16),
            pltpu.VMEM((edges, features), BF16),
            pltpu.VMEM((edges, features), BF16),
        ],
    )(
        place, recv_rows, send_own, hot, preact_own, grad_msg, near(edge_lat),
        near(weight_send), near(weight_out), *map(near, borrowed),
    )

    own_sums, recv_sums, *back = call(
        sums_body, [node_sum, node_sum] + [block] * rounds, [SMEM] + [VMEM] * 3
    )(edge_recv_block, edge_src, recv_node, grad_preact)
    returned = [swap(back[section], bits[section]) for section in range(rounds)]

    def axis_of(bit):
        return split[0] if bit == "part" else bits[bit]

    def halves(rows):
        return [((rows // 2, features), F32), ((rows // 2, features), BF16)]

    got = swap(give, bits[0])
    flows = call(
        functools.partial(split_body, colours), halves(half // colours) * colours, [VMEM] * 2
    )(keep, near(got))
    depth = len(orders[0])
    level = 0
    rows = half // colours // 2
    flows = [(flows[2 * colour], flows[2 * colour + 1], order) for colour, order in enumerate(orders)]
    while True:
        pairs = []
        for keep, give, order in flows:
            pairs += [keep, near(swap(give, axis_of(order[level])))]
        level += 1
        if level == depth:
            break
        merged = len(flows) if level == colours else 1
        if len(flows) == 2 and merged == 1:
            flows = [
                (*call(functools.partial(split_body, 1), halves(rows), [VMEM] * 2)(*pairs[2 * colour : 2 * colour + 2]), order)
                for colour, (_, _, order) in enumerate(flows)
            ]
            rows //= 2
        else:
            keep, give = call(
                functools.partial(merge_body, merged, size), halves(rows * merged), [VMEM] * (2 * merged)
            )(*pairs)
            flows = [(keep, give, orders[0])]
            rows = rows * merged // 2
    (total,) = call(round_body, [((rows, features), BF16)], [VMEM] * 2)(*pairs)
    for axis in traj_axes[len(split) :]:
        (total,) = call(round_body, [((rows, features), BF16)], [VMEM] * 2)(
            total, near(swap(total, axis))
        )
    parts = [total] + [near(swap(total, axis)) for axis in split]
    (weight_grads,) = call(
        finish_body, [((4 * share, features), F32)], [SMEM] + [VMEM] * len(parts), kept=False
    )(place, *parts)
    agg, grad_edges = call(
        edge_body, [((nodes, features), BF16), wide], [SMEM] + [VMEM] * 5, kept=False
    )(edge_recv_block, recv_node, grad_preact, message, grad_edge, weight_edge)
    (grad_nodes,) = call(
        node_body,
        [((nodes, features), BF16)],
        [SMEM] + [VMEM] * (4 + rounds),
        kept=False,
        scratch=[pltpu.VMEM((nodes, features), F32)],
    )(send_blocks, own_sums, recv_sums, weight_send, weight_recv, *map(near, returned))
    return agg[None], grad_edges[None], grad_nodes[None], weight_grads.reshape(4, share, features)


def solution(mesh):
    traj_axes = tuple(f"t{bit}" for bit in reversed(range(mesh.shape["traj"].bit_length() - 1)))
    dom_axes = tuple(f"d{bit}" for bit in reversed(range(mesh.shape["dom"].bit_length() - 1)))
    names = traj_axes + dom_axes
    bit_mesh = Mesh(mesh.devices.reshape((2,) * len(names)), names)
    rows = P(traj_axes, dom_axes, None)
    in_specs = (rows,) * 4 + (P(),) * 4 + (P(dom_axes),) * 4
    out_specs = (rows,) * 3 + (P(None, dom_axes, None),)

    def body(*arrays):
        return per_device(traj_axes, dom_axes, *arrays)

    return jax.shard_map(
        body, mesh=bit_mesh, in_specs=in_specs, out_specs=out_specs, check_vma=False
    )
```

```python
import functools

import jax
import jax.numpy as jnp
from jax import lax
from jax.experimental import pallas as pl
from jax.experimental.pallas import tpu as pltpu
from jax.sharding import Mesh, PartitionSpec as P


LANES = 128
ROOM = 24 << 20
BF16 = jnp.bfloat16
F32 = jnp.float32
VMEM = pl.BlockSpec(memory_space=pltpu.VMEM)
SMEM = pl.BlockSpec(memory_space=pltpu.SMEM)


def dot(former, latter):
    return jnp.dot(former, latter, preferred_element_type=F32)


def dot_rows(former, latter):
    return lax.dot_general(former, latter, (((0,), (0,)), ((), ())), preferred_element_type=F32)


def dot_cols(former, latter):
    return lax.dot_general(former, latter, (((1,), (1,)), ((), ())), preferred_element_type=F32)


def near(array):
    return pltpu.with_memory_space_constraint(array, pltpu.VMEM)


def far(array):
    return pltpu.with_memory_space_constraint(array, pltpu.HBM)


def call(body, outs, ins, kept=True, scratch=()):
    fresh = pltpu.VMEM if kept else jax.ShapeDtypeStruct
    return pl.pallas_call(
        body,
        out_shape=[fresh(shape, kind) for shape, kind in outs],
        in_specs=ins,
        out_specs=[VMEM] * len(outs),
        scratch_shapes=scratch,
        compiler_params=pltpu.CompilerParams(vmem_limit_bytes=ROOM),
    )


def swap(array, axis):
    return lax.ppermute(array, axis, [(0, 1), (1, 0)])


def down_rows(row, count):
    return jnp.transpose(jnp.broadcast_to(row, (LANES, count)))


def onehot_cols(index_cols, first, blocks):
    lane = lax.broadcasted_iota(jnp.int32, index_cols.shape, 1)
    parts = [
        jnp.where(index_cols == lane + (first + LANES * block), 1.0, 0.0).astype(BF16)
        for block in range(blocks)
    ]
    return jnp.concatenate(parts, axis=1)


def onehot_rows(index_row, first, rows):
    node = lax.broadcasted_iota(jnp.int32, (rows, index_row.shape[1]), 0) + first
    return jnp.where(node == index_row, 1.0, 0.0).astype(BF16)


def receiver_row(recv_block, recv_node):
    edges = recv_node.shape[1]
    return jnp.concatenate(
        [
            recv_node[:, LANES * block : LANES * (block + 1)] + recv_block[block] * LANES
            for block in range(edges // LANES)
        ],
        axis=1,
    )


def pick_body(send_blocks, node_lat, *lent):
    for section, out in enumerate(lent):
        out[...] = node_lat[pl.ds(pl.multiple_of(send_blocks[section] * LANES, LANES), LANES), :]


def early_body(
    rounds, recv_block, edge_src, recv_node, node_lat, edge_lat, grad_edge, grad_agg, weight_edge,
    weight_recv, receiver_out, recv_out, send_out, hot_out, preact_out, grad_msg_out,
):
    nodes = node_lat.shape[0]
    edges = edge_lat.shape[0]
    row = receiver_row(recv_block, recv_node[...])
    receiver_out[...] = row
    receiver = down_rows(row, edges)
    sender = down_rows(edge_src[...], edges)
    hot_recv = onehot_cols(receiver, 0, nodes // LANES)
    recv_rows = dot(hot_recv, node_lat[...]).astype(BF16)
    recv_out[...] = recv_rows
    send_out[...] = dot(onehot_cols(sender, 0, nodes // LANES), node_lat[...]).astype(BF16)
    hot_out[...] = onehot_cols(sender, nodes, rounds)
    preact_out[...] = dot(edge_lat[...], weight_edge[...]) + dot(recv_rows, weight_recv[...])
    grad_msg_out[...] = grad_edge[...].astype(F32) + dot(hot_recv, grad_agg[...])


def main_body(
    rounds, send_own, hot, preact_own, grad_msg, weight_send, weight_out, *refs
):
    borrowed = refs[:rounds]
    send_out, hidden_out, grad_proj_out, grad_preact_out, message_out, table = refs[rounds:]
    edges = send_own.shape[0]
    for section in range(rounds):
        table[LANES * section : LANES * (section + 1), :] = borrowed[section][...]
    step = edges // 2
    for start in range(0, edges, step):
        rows = slice(start, start + step)
        send = (send_own[rows, :].astype(F32) + dot(hot[rows, :], table[...])).astype(BF16)
        send_out[rows, :] = send
        preact = preact_own[rows, :] + dot(send, weight_send[...])
        sigmoid = jax.nn.sigmoid(preact)
        hidden = (preact * sigmoid).astype(BF16)
        hidden_out[rows, :] = hidden
        slope = sigmoid * (1.0 + preact * (1.0 - sigmoid))
        projected = dot(hidden, weight_out[...])
        centered = projected - jnp.mean(projected, axis=1, keepdims=True)
        inv_std = lax.rsqrt(jnp.mean(centered * centered, axis=1, keepdims=True) + 1e-05)
        normed = centered * inv_std
        message_out[rows, :] = normed.astype(BF16)
        grad = grad_msg[rows, :]
        grad_proj = inv_std * (
            grad
            - jnp.mean(grad, axis=1, keepdims=True)
            - normed * jnp.mean(grad * normed, axis=1, keepdims=True)
        )
        grad_proj = grad_proj.astype(BF16)
        grad_proj_out[rows, :] = grad_proj
        grad_preact_out[rows, :] = (dot_cols(grad_proj, weight_out[...]) * slope).astype(BF16)


def place_of(split, dom_axes):
    domain = 0
    for axis in dom_axes:
        domain = domain * 2 + lax.axis_index(axis)
    return lax.axis_index(split[0]) if split else 0, domain


def pieces_of(plan, where, sums, side):
    part, own = where()
    for whiches, flip, domain in plan:
        owner = own ^ (domain | side)
        parts = [sums[which ^ (flip * part), owner] for which in whiches]
        yield parts[0] if len(parts) == 1 else jnp.concatenate(parts, axis=0)


def grads_body(plan, where, *refs):
    sums, give_out = refs[-2:]
    for which in range(sums.shape[0]):
        total = dot_rows(refs[2 * which][...], refs[2 * which + 1][...])
        sums[which] = total.reshape(sums.shape[1:])
    at = 0
    for piece in pieces_of(plan, where, sums, 1):
        give_out[at : at + piece.shape[0], :] = piece.astype(BF16)
        at += piece.shape[0]


def chip_body(plan, where, sums, got, keep_out, give_out):
    at = 0
    half = keep_out.shape[0]
    for piece in pieces_of(plan, where, sums, 0):
        rows = slice(at, at + piece.shape[0])
        target, first = (keep_out, at) if at < half else (give_out, at - half)
        total = piece + got[rows, :].astype(F32)
        target[first : first + piece.shape[0], :] = total.astype(target.dtype)
        at += piece.shape[0]


def sums_body(edge_src, receiver, grad_preact, own_out, recv_out, *back_out):
    nodes = own_out.shape[0]
    rounds = len(back_out)
    rows = grad_preact[...]
    slot_sums = dot(onehot_rows(edge_src[...], 0, nodes + rounds * LANES), rows)
    own_out[...] = slot_sums[:nodes]
    for section in range(rounds):
        first = nodes + LANES * section
        back_out[section][...] = slot_sums[first : first + LANES].astype(BF16)
    recv_out[...] = dot(onehot_rows(receiver[...], 0, nodes), rows)


def split_body(keep, got, keep_out, give_out):
    half = keep.shape[0] // 2
    for target, first in ((give_out, half), (keep_out, 0)):
        rows = slice(first, first + half)
        target[...] = (keep[rows, :] + got[rows, :].astype(F32)).astype(target.dtype)


def round_body(keep, got, out):
    out[...] = (keep[...] + got[...].astype(F32)).astype(BF16)


def finish_body(colours, where, *refs):
    *parts, out = refs
    own, _ = where()
    take = parts[0].shape[0]
    for index, part in enumerate(parts):
        flip, colour = divmod(index, colours)
        first = pl.multiple_of(((own ^ flip) * colours + colour) * take, take)
        out[pl.ds(first, take), :] = part[...].astype(F32)


def edge_body(receiver, grad_preact, message, grad_edge, weight_edge, agg_out, edge_out):
    agg_out[...] = dot(onehot_rows(receiver[...], 0, agg_out.shape[0]), message[...]).astype(BF16)
    edge_out[...] = (
        grad_edge[...].astype(F32) + dot_cols(grad_preact[...], weight_edge[...])
    ).astype(BF16)


def dot_cols_split(former, latter):
    high = former.astype(BF16)
    low = (former - high.astype(F32)).astype(BF16)
    return dot_cols(high, latter) + dot_cols(low, latter)


def node_body(send_blocks, own_sums, recv_sums, weight_send, weight_recv, *refs):
    returned, out, total = refs[:-2], refs[-2], refs[-1]
    for first in range(0, out.shape[0], LANES):
        rows = slice(first, first + LANES)
        summed = own_sums[rows, :]
        for section, block in enumerate(returned):
            mine = send_blocks[:, section : section + 1] == first // LANES
            summed = summed + jnp.where(mine, block[...].astype(F32), 0.0)
        total[rows, :] = summed
    out[...] = (
        dot_cols_split(total[...], weight_send[...])
        + dot_cols_split(recv_sums[...], weight_recv[...])
    ).astype(BF16)


def layout(share, parts, tops):
    colours = 2 if parts == 2 and tops and share >= 16 else 1
    per_part = 4 // parts
    orders = [(["part"] if parts == 2 else []) + list(range(1, tops + 1))]
    if colours == 2:
        orders.append([1, "part"] + list(range(2, tops + 1)))
    plans = []
    for order in orders:
        pieces = []
        for index in range(2 ** len(order)):
            domain, flip = 0, 0
            for level, bit in enumerate(order):
                on = index >> (len(order) - 1 - level) & 1
                if bit == "part":
                    flip = on
                else:
                    domain |= on << bit
            count = per_part // colours
            pieces.append((tuple(which ^ (flip * count) for which in range(count)), count, domain))
        plans.append(tuple(pieces))
    return plans, orders


def per_device(
    traj_axes, dom_axes, node_lat, edge_lat, grad_edge, grad_agg, weight_edge, weight_send,
    weight_recv, weight_out, edge_src, edge_recv_block, edge_recv_node, send_blocks,
):
    node_lat, edge_lat, grad_edge, grad_agg = node_lat[0], edge_lat[0], grad_edge[0], grad_agg[0]
    nodes, features = node_lat.shape
    edges = edge_lat.shape[0]
    rounds = send_blocks.shape[0]
    edge_src = edge_src.reshape(1, edges)
    recv_node = edge_recv_node.reshape(1, edges)
    bits = dom_axes[::-1]
    share = features // 2 ** len(bits)
    split = traj_axes[:1] if 2 * share >= 16 else ()
    plans, orders = layout(share, 1 + len(split), len(bits) - 1)
    colours = len(orders)
    half = 2 * features
    wide = ((edges, features), BF16)
    wide_sum = ((edges, features), F32)
    node_sum = ((nodes, features), F32)
    block = ((LANES, features), BF16)
    where = functools.partial(place_of, split, dom_axes)

    lent = call(pick_body, [block] * rounds, [SMEM, VMEM])(
        far(send_blocks), far(node_lat)
    )
    borrowed = [swap(lent[section], bits[section]) for section in range(rounds)]
    receiver, recv_rows, send_own, hot, preact_own, grad_msg = call(
        functools.partial(early_body, rounds),
        [((1, edges), jnp.int32), wide, wide, ((edges, rounds * LANES), BF16), wide_sum, wide_sum],
        [SMEM] + [VMEM] * 8,
    )(
        *map(far, (edge_recv_block, edge_src, recv_node, node_lat, edge_lat)),
        *map(far, (grad_edge, grad_agg, weight_edge, weight_recv)),
    )
    send_rows, hidden, grad_proj, grad_preact, message = call(
        functools.partial(main_body, rounds),
        [wide] * 5,
        [VMEM] * (6 + rounds),
        scratch=[pltpu.VMEM((rounds * LANES, features), BF16)],
    )(
        send_own, hot, preact_own, grad_msg, near(weight_send), near(weight_out),
        *map(near, borrowed),
    )

    factors = [
        (near(edge_lat), grad_preact), (send_rows, grad_preact), (recv_rows, grad_preact),
        (hidden, grad_proj),
    ]
    rows = half // colours
    flows = [None] * colours
    for colour in reversed(range(colours)):
        used = factors[colour::colours]
        sums, give = call(
            functools.partial(grads_body, plans[colour], where),
            [((len(used), 2 ** len(bits), share, features), F32), ((rows, features), BF16)],
            [VMEM] * (2 * len(used)),
        )(*sum(used, ()))
        flows[colour] = (sums, near(swap(give, bits[0])))

    own_sums, recv_sums, *back = call(
        sums_body, [node_sum, node_sum] + [block] * rounds, [VMEM] * 3
    )(near(edge_src), receiver, grad_preact)
    returned = [swap(back[section], bits[section]) for section in range(rounds)]

    def halves(rows):
        return [((rows, features), F32), ((rows, features), BF16)]

    for level in range(len(orders[0])):
        rows //= 2
        for colour, order in enumerate(orders):
            if level:
                fold = call(split_body, halves(rows), [VMEM] * 2)
            else:
                body = functools.partial(chip_body, plans[colour], where)
                fold = call(body, halves(rows), [VMEM] * 2)
            keep, give = fold(*flows[colour])
            axis = split[0] if order[level] == "part" else bits[order[level]]
            flows[colour] = (keep, near(swap(give, axis)))
    totals = []
    for flow in flows:
        (total,) = call(round_body, [((rows, features), BF16)], [VMEM] * 2)(*flow)
        for axis in traj_axes[len(split) :]:
            (total,) = call(round_body, [((rows, features), BF16)], [VMEM] * 2)(
                total, near(swap(total, axis))
            )
        totals.append(total)
    totals += [near(swap(total, axis)) for axis in split for total in totals]
    (weight_grads,) = call(
        functools.partial(finish_body, colours, where),
        [((4 * share, features), F32)],
        [VMEM] * len(totals),
        kept=False,
    )(*totals)
    agg, grad_edges = call(
        edge_body, [((nodes, features), BF16), wide], [VMEM] * 5, kept=False
    )(receiver, grad_preact, message, near(grad_edge), near(weight_edge))
    (grad_nodes,) = call(
        node_body,
        [((nodes, features), BF16)],
        [VMEM] * (5 + rounds),
        kept=False,
        scratch=[pltpu.VMEM((nodes, features), F32)],
    )(
        near(send_blocks.reshape(1, rounds)), own_sums, recv_sums, near(weight_send), near(weight_recv),
        *map(near, returned),
    )
    return agg[None], grad_edges[None], grad_nodes[None], weight_grads.reshape(4, share, features)


def solution(mesh):
    traj_axes = tuple(f"t{bit}" for bit in reversed(range(mesh.shape["traj"].bit_length() - 1)))
    dom_axes = tuple(f"d{bit}" for bit in reversed(range(mesh.shape["dom"].bit_length() - 1)))
    names = traj_axes + dom_axes
    bit_mesh = Mesh(mesh.devices.reshape((2,) * len(names)), names)
    rows = P(traj_axes, dom_axes, None)
    in_specs = (rows,) * 4 + (P(),) * 4 + (P(dom_axes),) * 4
    out_specs = (rows,) * 3 + (P(None, dom_axes, None),)

    def body(*arrays):
        return per_device(traj_axes, dom_axes, *arrays)

    return jax.shard_map(
        body, mesh=bit_mesh, in_specs=in_specs, out_specs=out_specs, check_vma=False
    )
```

```python
import functools

import jax
import jax.numpy as jnp
from jax import lax
from jax.experimental import pallas as pl
from jax.experimental.pallas import tpu as pltpu
from jax.sharding import Mesh, PartitionSpec as P


LANES = 128
ROOM = 24 << 20
BF16 = jnp.bfloat16
F32 = jnp.float32
VMEM = pl.BlockSpec(memory_space=pltpu.VMEM)
SMEM = pl.BlockSpec(memory_space=pltpu.SMEM)


def dot(former, latter):
    return jnp.dot(former, latter, preferred_element_type=F32)


def dot_rows(former, latter):
    return lax.dot_general(former, latter, (((0,), (0,)), ((), ())), preferred_element_type=F32)


def dot_cols(former, latter):
    return lax.dot_general(former, latter, (((1,), (1,)), ((), ())), preferred_element_type=F32)


def near(array):
    return pltpu.with_memory_space_constraint(array, pltpu.VMEM)


def far(array):
    return pltpu.with_memory_space_constraint(array, pltpu.HBM)


def call(body, outs, ins, kept=True, scratch=()):
    fresh = pltpu.VMEM if kept else jax.ShapeDtypeStruct
    return pl.pallas_call(
        body,
        out_shape=[fresh(shape, kind) for shape, kind in outs],
        in_specs=ins,
        out_specs=[VMEM] * len(outs),
        scratch_shapes=scratch,
        compiler_params=pltpu.CompilerParams(vmem_limit_bytes=ROOM),
    )


def swap(array, axis):
    return lax.ppermute(array, axis, [(0, 1), (1, 0)])


def down_rows(row, count):
    return jnp.transpose(jnp.broadcast_to(row, (LANES, count)))


def onehot_cols(index_cols, first, blocks):
    lane = lax.broadcasted_iota(jnp.int32, index_cols.shape, 1)
    parts = [
        jnp.where(index_cols == lane + (first + LANES * block), 1.0, 0.0).astype(BF16)
        for block in range(blocks)
    ]
    return jnp.concatenate(parts, axis=1)


def onehot_rows(index_row, first, rows):
    node = lax.broadcasted_iota(jnp.int32, (rows, index_row.shape[1]), 0) + first
    return jnp.where(node == index_row, 1.0, 0.0).astype(BF16)


def receiver_row(recv_block, recv_node):
    edges = recv_node.shape[1]
    return jnp.concatenate(
        [
            recv_node[:, LANES * block : LANES * (block + 1)] + recv_block[block] * LANES
            for block in range(edges // LANES)
        ],
        axis=1,
    )


def pick_body(send_blocks, node_lat, *lent):
    for section, out in enumerate(lent):
        out[...] = node_lat[pl.ds(pl.multiple_of(send_blocks[section] * LANES, LANES), LANES), :]


def early_body(
    rounds, recv_block, send_blocks, edge_src, recv_node, node_lat, edge_lat, grad_edge, grad_agg, weight_edge,
    weight_recv, blocks_out, sender_out, receiver_out, edge_out, recv_out, send_out, hot_out,
    preact_out, grad_msg_out,
):
    nodes = node_lat.shape[0]
    edges = edge_lat.shape[0]
    row = receiver_row(recv_block, recv_node[...])
    receiver_out[...] = row
    blocks_out[...] = send_blocks[...]
    sender_out[...] = edge_src[...]
    edge_out[...] = edge_lat[...]
    receiver = down_rows(row, edges)
    sender = down_rows(edge_src[...], edges)
    hot_recv = onehot_cols(receiver, 0, nodes // LANES)
    recv_rows = dot(hot_recv, node_lat[...]).astype(BF16)
    recv_out[...] = recv_rows
    send_out[...] = dot(onehot_cols(sender, 0, nodes // LANES), node_lat[...]).astype(BF16)
    hot_out[...] = onehot_cols(sender, nodes, rounds)
    preact_out[...] = dot(edge_lat[...], weight_edge[...]) + dot(recv_rows, weight_recv[...])
    grad_msg_out[...] = grad_edge[...].astype(F32) + dot(hot_recv, grad_agg[...])


def place_of(split, dom_axes):
    domain = 0
    for axis in dom_axes:
        domain = domain * 2 + lax.axis_index(axis)
    return lax.axis_index(split[0]) if split else 0, domain


def store_rows(target, at, blocks):
    run = []
    for block in blocks:
        run.append(block)
        rows = sum(part.shape[0] for part in run)
        if rows % 16 == 0:
            whole = run[0] if len(run) == 1 else jnp.concatenate(run, axis=0)
            target[at : at + rows, :] = whole.astype(target.dtype)
            at += rows
            run = []


def give_rows(domains, where, sums, give_out):
    _, own = where()
    store_rows(give_out, 0, [sums[own ^ (domain | 1)] for domain in domains])


def main_body(
    rounds, domains, where, send_own, hot, preact_own, grad_msg, weight_send, weight_out, *refs
):
    borrowed = refs[:rounds]
    send_out, grad_preact_out, message_out, sums_out, give_out, table = refs[rounds:]
    for section in range(rounds):
        table[LANES * section : LANES * (section + 1), :] = borrowed[section][...]
    send = (send_own[...].astype(F32) + dot(hot[...], table[...])).astype(BF16)
    send_out[...] = send
    preact = preact_own[...] + dot(send, weight_send[...])
    sigmoid = jax.nn.sigmoid(preact)
    hidden = (preact * sigmoid).astype(BF16)
    slope = sigmoid * (1.0 + preact * (1.0 - sigmoid))
    projected = dot(hidden, weight_out[...])
    centered = projected - jnp.mean(projected, axis=1, keepdims=True)
    inv_std = lax.rsqrt(jnp.mean(centered * centered, axis=1, keepdims=True) + 1e-05)
    normed = centered * inv_std
    message_out[...] = normed.astype(BF16)
    grad = grad_msg[...]
    grad_proj = inv_std * (
        grad
        - jnp.mean(grad, axis=1, keepdims=True)
        - normed * jnp.mean(grad * normed, axis=1, keepdims=True)
    )
    grad_proj = grad_proj.astype(BF16)
    grad_preact_out[...] = (dot_cols(grad_proj, weight_out[...]) * slope).astype(BF16)
    sums_out[...] = dot_rows(hidden, grad_proj).reshape(sums_out.shape)
    give_rows(domains, where, sums_out, give_out)


def grads_body(domains, where, former, latter, sums_out, give_out):
    sums_out[...] = dot_rows(former[...], latter[...]).reshape(sums_out.shape)
    give_rows(domains, where, sums_out, give_out)


def chip_body(plan, parts, where, *refs):
    keep_out, give_out = refs[-2:]
    sums, gots = refs[0:-2:2], refs[1:-2:2]
    count = len(sums) // parts
    part, own = where()
    half = len(plan) // 2

    def add(which, index, domain):
        share = sums[which].shape[1]
        first = index * share
        start = first // 16 * 16
        got = gots[which][start : start + max(share, 16), :].astype(F32)
        return sums[which][own ^ domain] + got[first - start : first - start + share]

    for this in range(parts):

        @pl.when(part == this)
        def _():
            for target, pieces in ((give_out, plan[half:]), (keep_out, plan[:half])):
                store_rows(
                    target,
                    0,
                    [
                        add((this ^ flip) * count + which, index, domain)
                        for flip, index, domain in pieces
                        for which in range(count)
                    ],
                )


def sums_body(edge_src, receiver, grad_preact, own_out, recv_out, *back_out):
    nodes = own_out.shape[0]
    rounds = len(back_out)
    rows = grad_preact[...]
    slot_sums = dot(onehot_rows(edge_src[...], 0, nodes + rounds * LANES), rows)
    own_out[...] = slot_sums[:nodes]
    for section in range(rounds):
        first = nodes + LANES * section
        back_out[section][...] = slot_sums[first : first + LANES].astype(BF16)
    recv_out[...] = dot(onehot_rows(receiver[...], 0, nodes), rows)


def split_body(keep, got, keep_out, give_out):
    half = keep.shape[0] // 2
    for target, first in ((give_out, half), (keep_out, 0)):
        rows = slice(first, first + half)
        target[...] = (keep[rows, :] + got[rows, :].astype(F32)).astype(target.dtype)


def round_body(keep, got, out):
    out[...] = (keep[...] + got[...].astype(F32)).astype(BF16)


def finish_body(colours, where, *refs):
    *parts, out = refs
    own, _ = where()
    take = parts[0].shape[0]
    for index, part in enumerate(parts):
        flip, colour = divmod(index, colours)
        first = pl.multiple_of(((own ^ flip) * colours + colour) * take, take)
        out[pl.ds(first, take), :] = part[...].astype(F32)


def edge_body(receiver, grad_preact, message, grad_edge, weight_edge, agg_out, edge_out):
    agg_out[...] = dot(onehot_rows(receiver[...], 0, agg_out.shape[0]), message[...]).astype(BF16)
    edge_out[...] = (
        grad_edge[...].astype(F32) + dot_cols(grad_preact[...], weight_edge[...])
    ).astype(BF16)


def dot_cols_split(former, latter):
    high = former.astype(BF16)
    low = (former - high.astype(F32)).astype(BF16)
    return dot_cols(high, latter) + dot_cols(low, latter)


def node_body(send_blocks, own_sums, recv_sums, weight_send, weight_recv, *refs):
    returned, out, total = refs[:-2], refs[-2], refs[-1]
    for first in range(0, out.shape[0], LANES):
        rows = slice(first, first + LANES)
        summed = own_sums[rows, :]
        for section, block in enumerate(returned):
            mine = send_blocks[:, section : section + 1] == first // LANES
            summed = summed + jnp.where(mine, block[...].astype(F32), 0.0)
        total[rows, :] = summed
    out[...] = (
        dot_cols_split(total[...], weight_send[...])
        + dot_cols_split(recv_sums[...], weight_recv[...])
    ).astype(BF16)


def layout(share, parts, tops):
    colours = 2 if parts == 2 and tops and share >= 16 else 1
    orders = [(["part"] if parts == 2 else []) + list(range(1, tops + 1))]
    if colours == 2:
        orders.append([1, "part"] + list(range(2, tops + 1)))
    domains = [index << 1 for index in range(2**tops)]
    plans = []
    for order in orders:
        pieces = []
        for index in range(2 ** len(order)):
            domain, flip = 0, 0
            for level, bit in enumerate(order):
                on = index >> (len(order) - 1 - level) & 1
                if bit == "part":
                    flip = on
                else:
                    domain |= on << bit
            pieces.append((flip, domain >> 1, domain))
        plans.append(pieces)
    return plans, orders, domains


def per_device(
    traj_axes, dom_axes, node_lat, edge_lat, grad_edge, grad_agg, weight_edge, weight_send,
    weight_recv, weight_out, edge_src, edge_recv_block, edge_recv_node, send_blocks,
):
    node_lat, edge_lat, grad_edge, grad_agg = node_lat[0], edge_lat[0], grad_edge[0], grad_agg[0]
    nodes, features = node_lat.shape
    edges = edge_lat.shape[0]
    rounds = send_blocks.shape[0]
    edge_src = edge_src.reshape(1, edges)
    recv_node = edge_recv_node.reshape(1, edges)
    bits = dom_axes[::-1]
    share = features // 2 ** len(bits)
    split = traj_axes[:1] if 2 * share >= 16 else ()
    plans, orders, domains = layout(share, 1 + len(split), len(bits) - 1)
    colours = len(orders)
    half = 2 * features
    wide = ((edges, features), BF16)
    wide_sum = ((edges, features), F32)
    node_sum = ((nodes, features), F32)
    block = ((LANES, features), BF16)
    where = functools.partial(place_of, split, dom_axes)

    lent = call(pick_body, [block] * rounds, [SMEM, VMEM])(
        far(send_blocks), far(node_lat)
    )
    borrowed = [swap(lent[section], bits[section]) for section in range(rounds)]
    blocks, sender, receiver, edge_rows, recv_rows, send_own, hot, preact_own, grad_msg = call(
        functools.partial(early_body, rounds),
        [((1, rounds), jnp.int32)] + [((1, edges), jnp.int32)] * 2 + [wide, wide, wide, ((edges, rounds * LANES), BF16), wide_sum, wide_sum],
        [SMEM] + [VMEM] * 9,
    )(
        *map(far, (edge_recv_block, send_blocks.reshape(1, rounds), edge_src, recv_node)),
        *map(far, (node_lat, edge_lat)),
        *map(far, (grad_edge, grad_agg, weight_edge, weight_recv)),
    )
    sum_rows = [
        ((2 ** len(bits), share, features), F32), ((share * len(domains), features), BF16)
    ]
    sums, gives = [None] * 4, [None] * 4
    send_rows, grad_preact, message, sums[3], gives[3] = call(
        functools.partial(main_body, rounds, domains, where),
        [wide] * 3 + sum_rows,
        [VMEM] * (6 + rounds),
        scratch=[pltpu.VMEM((rounds * LANES, features), BF16)],
    )(
        send_own, hot, preact_own, grad_msg, near(weight_send), near(weight_out),
        *map(near, borrowed),
    )
    for which, rows in ((1, send_rows), (0, edge_rows), (2, recv_rows)):
        sums[which], gives[which] = call(
            functools.partial(grads_body, domains, where), sum_rows, [VMEM] * 2
        )(rows, grad_preact)
    gots = [near(swap(give, bits[0])) for give in gives]
    flows = [sum(zip(sums[colour::colours], gots[colour::colours]), ()) for colour in range(colours)]
    rows = half // colours

    own_sums, recv_sums, *back = call(
        sums_body, [node_sum, node_sum] + [block] * rounds, [VMEM] * 3
    )(sender, receiver, grad_preact)
    returned = [swap(back[section], bits[section]) for section in range(rounds)]

    def halves(rows):
        return [((rows, features), F32), ((rows, features), BF16)]

    for level in range(len(orders[0])):
        rows //= 2
        for colour, order in enumerate(orders):
            if level:
                fold = call(split_body, halves(rows), [VMEM] * 2)
            else:
                body = functools.partial(chip_body, plans[colour], 1 + len(split), where)
                fold = call(body, halves(rows), [VMEM] * len(flows[colour]))
            keep, give = fold(*flows[colour])
            axis = split[0] if order[level] == "part" else bits[order[level]]
            flows[colour] = (keep, near(swap(give, axis)))
    totals = []
    for flow in flows:
        (total,) = call(round_body, [((rows, features), BF16)], [VMEM] * 2)(*flow)
        for axis in traj_axes[len(split) :]:
            (total,) = call(round_body, [((rows, features), BF16)], [VMEM] * 2)(total, near(swap(total, axis)))
        totals.append(total)
    totals += [near(swap(total, axis)) for axis in split for total in totals]
    (weight_grads,) = call(
        functools.partial(finish_body, colours, where), [((4 * share, features), F32)], [VMEM] * len(totals), kept=False
    )(*totals)
    agg, grad_edges = call(
        edge_body, [((nodes, features), BF16), wide], [VMEM] * 5, kept=False
    )(receiver, grad_preact, message, near(grad_edge), near(weight_edge))
    (grad_nodes,) = call(
        node_body,
        [((nodes, features), BF16)],
        [VMEM] * (5 + rounds),
        kept=False,
        scratch=[pltpu.VMEM((nodes, features), F32)],
    )(
        blocks, own_sums, recv_sums, near(weight_send), near(weight_recv),
        *map(near, returned),
    )
    return agg[None], grad_edges[None], grad_nodes[None], weight_grads.reshape(4, share, features)


def solution(mesh):
    traj_axes = tuple(f"t{bit}" for bit in reversed(range(mesh.shape["traj"].bit_length() - 1)))
    dom_axes = tuple(f"d{bit}" for bit in reversed(range(mesh.shape["dom"].bit_length() - 1)))
    names = traj_axes + dom_axes
    bit_mesh = Mesh(mesh.devices.reshape((2,) * len(names)), names)
    rows = P(traj_axes, dom_axes, None)
    in_specs = (rows,) * 4 + (P(),) * 4 + (P(dom_axes),) * 4
    out_specs = (rows,) * 3 + (P(None, dom_axes, None),)

    def body(*arrays):
        return per_device(traj_axes, dom_axes, *arrays)

    return jax.shard_map(
        body, mesh=bit_mesh, in_specs=in_specs, out_specs=out_specs, check_vma=False
    )
```

```python
import functools

import jax
import jax.numpy as jnp
from jax import lax
from jax.experimental import pallas as pl
from jax.experimental.pallas import tpu as pltpu
from jax.sharding import Mesh, PartitionSpec as P


LANES = 128
ROOM = 24 << 20
BF16 = jnp.bfloat16
F32 = jnp.float32
VMEM = pl.BlockSpec(memory_space=pltpu.VMEM)
SMEM = pl.BlockSpec(memory_space=pltpu.SMEM)


def dot(former, latter):
    return jnp.dot(former, latter, preferred_element_type=F32)


def dot_rows(former, latter):
    return lax.dot_general(former, latter, (((0,), (0,)), ((), ())), preferred_element_type=F32)


def dot_cols(former, latter):
    return lax.dot_general(former, latter, (((1,), (1,)), ((), ())), preferred_element_type=F32)


def near(array):
    return pltpu.with_memory_space_constraint(array, pltpu.VMEM)


def far(array):
    return pltpu.with_memory_space_constraint(array, pltpu.HBM)


def call(body, outs, ins, kept=True, scratch=()):
    fresh = pltpu.VMEM if kept else jax.ShapeDtypeStruct
    return pl.pallas_call(
        body,
        out_shape=[fresh(shape, kind) for shape, kind in outs],
        in_specs=ins,
        out_specs=[VMEM] * len(outs),
        scratch_shapes=scratch,
        compiler_params=pltpu.CompilerParams(vmem_limit_bytes=ROOM),
    )


def swap(array, axis):
    return lax.ppermute(array, axis, [(0, 1), (1, 0)])


def down_rows(row, count):
    return jnp.transpose(jnp.broadcast_to(row, (LANES, count)))


def onehot_cols(index_cols, first, blocks):
    lane = lax.broadcasted_iota(jnp.int32, index_cols.shape, 1)
    parts = [
        jnp.where(index_cols == lane + (first + LANES * block), 1.0, 0.0).astype(BF16)
        for block in range(blocks)
    ]
    return jnp.concatenate(parts, axis=1)


def onehot_rows(index_row, first, rows):
    node = lax.broadcasted_iota(jnp.int32, (rows, index_row.shape[1]), 0) + first
    return jnp.where(node == index_row, 1.0, 0.0).astype(BF16)


def receiver_row(recv_block, recv_node):
    edges = recv_node.shape[1]
    return jnp.concatenate(
        [
            recv_node[:, LANES * block : LANES * (block + 1)] + recv_block[block] * LANES
            for block in range(edges // LANES)
        ],
        axis=1,
    )


def pick_body(send_blocks, node_lat, *lent):
    for section, out in enumerate(lent):
        out[...] = node_lat[pl.ds(pl.multiple_of(send_blocks[section] * LANES, LANES), LANES), :]


def early_body(
    rounds, recv_block, send_blocks, edge_src, recv_node, node_lat, edge_lat, grad_edge, grad_agg, weight_edge,
    weight_recv, blocks_out, sender_out, receiver_out, edge_out, recv_out, send_out, hot_out,
    preact_out, grad_msg_out,
):
    nodes = node_lat.shape[0]
    edges = edge_lat.shape[0]
    row = receiver_row(recv_block, recv_node[...])
    receiver_out[...] = row
    blocks_out[...] = send_blocks[...]
    sender_out[...] = edge_src[...]
    edge_out[...] = edge_lat[...]
    receiver = down_rows(row, edges)
    sender = down_rows(edge_src[...], edges)
    hot_recv = onehot_cols(receiver, 0, nodes // LANES)
    recv_rows = dot(hot_recv, node_lat[...]).astype(BF16)
    recv_out[...] = recv_rows
    send_out[...] = dot(onehot_cols(sender, 0, nodes // LANES), node_lat[...]).astype(BF16)
    hot_out[...] = onehot_cols(sender, nodes, rounds)
    preact_out[...] = dot(edge_lat[...], weight_edge[...]) + dot(recv_rows, weight_recv[...])
    grad_msg_out[...] = grad_edge[...].astype(F32) + dot(hot_recv, grad_agg[...])


def place_of(split, dom_axes):
    domain = 0
    for axis in dom_axes:
        domain = domain * 2 + lax.axis_index(axis)
    return lax.axis_index(split[0]) if split else 0, domain


def store_rows(target, at, blocks):
    run = []
    for block in blocks:
        run.append(block)
        rows = sum(part.shape[0] for part in run)
        if rows % 16 == 0:
            whole = run[0] if len(run) == 1 else jnp.concatenate(run, axis=0)
            target[at : at + rows, :] = whole.astype(target.dtype)
            at += rows
            run = []


def give_rows(domains, where, sums, give_out, at=0):
    _, own = where()
    store_rows(give_out, at, [sums[own ^ (domain | 1)] for domain in domains])


def main_body(
    rounds, domains, where, send_own, hot, preact_own, grad_msg, weight_send, weight_out, *refs
):
    borrowed = refs[:rounds]
    send_out, grad_preact_out, message_out, sums_out, give_out, table = refs[rounds:]
    for section in range(rounds):
        table[LANES * section : LANES * (section + 1), :] = borrowed[section][...]
    send = (send_own[...].astype(F32) + dot(hot[...], table[...])).astype(BF16)
    send_out[...] = send
    preact = preact_own[...] + dot(send, weight_send[...])
    sigmoid = jax.nn.sigmoid(preact)
    hidden = (preact * sigmoid).astype(BF16)
    slope = sigmoid * (1.0 + preact * (1.0 - sigmoid))
    projected = dot(hidden, weight_out[...])
    centered = projected - jnp.mean(projected, axis=1, keepdims=True)
    inv_std = lax.rsqrt(jnp.mean(centered * centered, axis=1, keepdims=True) + 1e-05)
    normed = centered * inv_std
    message_out[...] = normed.astype(BF16)
    grad = grad_msg[...]
    grad_proj = inv_std * (
        grad
        - jnp.mean(grad, axis=1, keepdims=True)
        - normed * jnp.mean(grad * normed, axis=1, keepdims=True)
    )
    grad_proj = grad_proj.astype(BF16)
    grad_preact_out[...] = (dot_cols(grad_proj, weight_out[...]) * slope).astype(BF16)
    sums_out[...] = dot_rows(hidden, grad_proj).reshape(sums_out.shape)
    give_rows(domains, where, sums_out, give_out)


def grads_body(domains, where, *refs):
    *sums_outs, give_out = refs[-(len(refs) // 3) - 1 :]
    for which, sums_out in enumerate(sums_outs):
        former, latter = refs[2 * which : 2 * which + 2]
        sums_out[...] = dot_rows(former[...], latter[...]).reshape(sums_out.shape)
        rows = give_out.shape[0] // len(sums_outs)
        give_rows(domains, where, sums_out, give_out, which * rows)


def chip_body(plan, parts, where, places, *refs):
    keep_out, give_out = refs[-2:]
    sums, gots = refs[: len(places)], refs[len(places) : -2]
    count = len(sums) // parts
    part, own = where()
    half = len(plan) // 2

    def add(which, index, domain):
        share = sums[which].shape[1]
        holder, first = places[which]
        first += index * share
        start = first // 16 * 16
        got = gots[holder][start : start + max(share, 16), :].astype(F32)
        return sums[which][own ^ domain] + got[first - start : first - start + share]

    def write(this):
        for target, pieces in ((give_out, plan[half:]), (keep_out, plan[:half])):
            store_rows(
                target,
                0,
                [
                    add((this ^ flip) * count + which, index, domain)
                    for flip, index, domain in pieces
                    for which in range(count)
                ],
            )

    if parts == 1:
        write(0)
    else:
        for this in range(parts):
            pl.when(part == this)(functools.partial(write, this))


def sums_body(edge_src, receiver, grad_preact, own_out, recv_out, *back_out):
    nodes = own_out.shape[0]
    rounds = len(back_out)
    rows = grad_preact[...]
    slot_sums = dot(onehot_rows(edge_src[...], 0, nodes + rounds * LANES), rows)
    own_out[...] = slot_sums[:nodes]
    for section in range(rounds):
        first = nodes + LANES * section
        back_out[section][...] = slot_sums[first : first + LANES].astype(BF16)
    recv_out[...] = dot(onehot_rows(receiver[...], 0, nodes), rows)


def split_body(keep, got, keep_out, give_out):
    half = keep.shape[0] // 2
    for target, first in ((give_out, half), (keep_out, 0)):
        rows = slice(first, first + half)
        target[...] = (keep[rows, :] + got[rows, :].astype(F32)).astype(target.dtype)


def round_body(keep, got, out):
    out[...] = (keep[...] + got[...].astype(F32)).astype(BF16)


def finish_body(where, *refs):
    *parts, out = refs
    own, _ = where()
    if len(parts) == 4:
        whole, split, whole_got, split_got = parts
        take = split.shape[0]
        total = whole[...].astype(F32) + whole_got[...].astype(F32)
        for half in range(2):
            out[2 * half * take : (2 * half + 1) * take, :] = total[half * take : (half + 1) * take]
        for flip, part in enumerate((split, split_got)):
            first = pl.multiple_of((2 * (own ^ flip) + 1) * take, take)
            out[pl.ds(first, take), :] = part[...].astype(F32)
    else:
        take = parts[0].shape[0]
        for flip, part in enumerate(parts):
            first = pl.multiple_of((own ^ flip) * take, take)
            out[pl.ds(first, take), :] = part[...].astype(F32)


def edge_body(receiver, grad_preact, message, grad_edge, weight_edge, agg_out, edge_out):
    agg_out[...] = dot(onehot_rows(receiver[...], 0, agg_out.shape[0]), message[...]).astype(BF16)
    edge_out[...] = (
        grad_edge[...].astype(F32) + dot_cols(grad_preact[...], weight_edge[...])
    ).astype(BF16)


def dot_cols_split(former, latter):
    high = former.astype(BF16)
    low = (former - high.astype(F32)).astype(BF16)
    return dot_cols(high, latter) + dot_cols(low, latter)


def node_body(send_blocks, own_sums, recv_sums, weight_send, weight_recv, *refs):
    returned, out, total = refs[:-2], refs[-2], refs[-1]
    for first in range(0, out.shape[0], LANES):
        rows = slice(first, first + LANES)
        summed = own_sums[rows, :]
        for section, block in enumerate(returned):
            mine = send_blocks[:, section : section + 1] == first // LANES
            summed = summed + jnp.where(mine, block[...].astype(F32), 0.0)
        total[rows, :] = summed
    out[...] = (
        dot_cols_split(total[...], weight_send[...])
        + dot_cols_split(recv_sums[...], weight_recv[...])
    ).astype(BF16)


def layout(share, parts, tops):
    colours = 2 if parts == 2 and tops and share >= 16 else 1
    orders = [(["part"] if parts == 2 else []) + list(range(1, tops + 1))]
    if colours == 2:
        orders.insert(0, list(range(1, tops + 1)))
    domains = [index << 1 for index in range(2**tops)]
    plans = []
    for order in orders:
        pieces = []
        for index in range(2 ** len(order)):
            domain, flip = 0, 0
            for level, bit in enumerate(order):
                on = index >> (len(order) - 1 - level) & 1
                if bit == "part":
                    flip = on
                else:
                    domain |= on << bit
            pieces.append((flip, domain >> 1, domain))
        plans.append(pieces)
    return plans, orders, domains


def per_device(
    traj_axes, dom_axes, node_lat, edge_lat, grad_edge, grad_agg, weight_edge, weight_send,
    weight_recv, weight_out, edge_src, edge_recv_block, edge_recv_node, send_blocks,
):
    node_lat, edge_lat, grad_edge, grad_agg = node_lat[0], edge_lat[0], grad_edge[0], grad_agg[0]
    nodes, features = node_lat.shape
    edges = edge_lat.shape[0]
    rounds = send_blocks.shape[0]
    edge_src = edge_src.reshape(1, edges)
    recv_node = edge_recv_node.reshape(1, edges)
    bits = dom_axes[::-1]
    share = features // 2 ** len(bits)
    split = traj_axes[:1] if 2 * share >= 16 else ()
    plans, orders, domains = layout(share, 1 + len(split), len(bits) - 1)
    colours = len(orders)
    half = 2 * features
    wide = ((edges, features), BF16)
    wide_sum = ((edges, features), F32)
    node_sum = ((nodes, features), F32)
    block = ((LANES, features), BF16)
    where = functools.partial(place_of, split, dom_axes)

    lent = call(pick_body, [block] * rounds, [SMEM, VMEM])(
        far(send_blocks), far(node_lat)
    )
    borrowed = [swap(lent[section], bits[section]) for section in range(rounds)]
    blocks, sender, receiver, edge_rows, recv_rows, send_own, hot, preact_own, grad_msg = call(
        functools.partial(early_body, rounds),
        [((1, rounds), jnp.int32)] + [((1, edges), jnp.int32)] * 2 + [wide, wide, wide, ((edges, rounds * LANES), BF16), wide_sum, wide_sum],
        [SMEM] + [VMEM] * 9,
    )(
        *map(far, (edge_recv_block, send_blocks.reshape(1, rounds), edge_src, recv_node)),
        *map(far, (node_lat, edge_lat)),
        *map(far, (grad_edge, grad_agg, weight_edge, weight_recv)),
    )
    sum_rows = [
        ((2 ** len(bits), share, features), F32), ((share * len(domains), features), BF16)
    ]
    sums, gives = [None] * 4, [None] * 4
    send_rows, grad_preact, message, sums[3], gives[3] = call(
        functools.partial(main_body, rounds, domains, where),
        [wide] * 3 + sum_rows,
        [VMEM] * (6 + rounds),
        scratch=[pltpu.VMEM((rounds * LANES, features), BF16)],
    )(
        send_own, hot, preact_own, grad_msg, near(weight_send), near(weight_out),
        *map(near, borrowed),
    )
    factors = {0: (edge_rows, grad_preact), 1: (send_rows, grad_preact), 2: (recv_rows, grad_preact)}
    gave = {(3,): gives[3]}
    for group in ((1,), (0, 2)):
        shape, (give_shape, kind) = sum_rows
        *made, gave[group] = call(
            functools.partial(grads_body, domains, where),
            [shape] * len(group) + [((give_shape[0] * len(group), features), kind)],
            [VMEM] * (2 * len(group)),
        )(*sum((factors[which] for which in group), ()))
        for which, array in zip(group, made):
            sums[which] = array
    came = {group: near(swap(give, bits[0])) for group, give in gave.items()}
    flows, places = [], []
    for colour in range(colours):
        used = range(4)[colour::colours]
        groups = [group for group in came if set(group) & set(used)]
        rows = share * len(domains)
        places.append(
            [
                (holder, group.index(which) * rows)
                for which in used
                for holder, group in enumerate(groups)
                if which in group
            ]
        )
        flows.append([sums[which] for which in used] + [came[group] for group in groups])
    rows = half // colours

    own_sums, recv_sums, *back = call(
        sums_body, [node_sum, node_sum] + [block] * rounds, [VMEM] * 3
    )(sender, receiver, grad_preact)
    returned = [swap(back[section], bits[section]) for section in range(rounds)]

    def halves(rows):
        return [((rows, features), F32), ((rows, features), BF16)]

    depths = [len(order) for order in orders]
    for level in range(max(depths)):
        rows //= 2
        for colour, order in enumerate(orders):
            if level >= depths[colour]:
                continue
            if level:
                fold = call(split_body, halves(rows), [VMEM] * 2)
            else:
                parts = 2 if "part" in order else 1
                body = functools.partial(chip_body, plans[colour], parts, where, places[colour])
                fold = call(body, halves(rows), [VMEM] * len(flows[colour]))
            keep, give = fold(*flows[colour])
            axis = split[0] if order[level] == "part" else bits[order[level]]
            flows[colour] = (keep, near(swap(give, axis)))
    totals = []
    for flow in flows:
        sized = [((flow[0].shape[0], features), BF16)]
        (total,) = call(round_body, sized, [VMEM] * 2)(*flow)
        for axis in traj_axes[len(split) :]:
            (total,) = call(round_body, sized, [VMEM] * 2)(total, near(swap(total, axis)))
        totals.append(total)
    totals += [near(swap(total, axis)) for axis in split for total in totals]
    (weight_grads,) = call(
        functools.partial(finish_body, where),
        [((4 * share, features), F32)],
        [VMEM] * len(totals),
        kept=False,
    )(*totals)
    agg, grad_edges = call(
        edge_body, [((nodes, features), BF16), wide], [VMEM] * 5, kept=False
    )(receiver, grad_preact, message, near(grad_edge), near(weight_edge))
    (grad_nodes,) = call(
        node_body,
        [((nodes, features), BF16)],
        [VMEM] * (5 + rounds),
        kept=False,
        scratch=[pltpu.VMEM((nodes, features), F32)],
    )(
        blocks, own_sums, recv_sums, near(weight_send), near(weight_recv),
        *map(near, returned),
    )
    return agg[None], grad_edges[None], grad_nodes[None], weight_grads.reshape(4, share, features)


def solution(mesh):
    traj_axes = tuple(f"t{bit}" for bit in reversed(range(mesh.shape["traj"].bit_length() - 1)))
    dom_axes = tuple(f"d{bit}" for bit in reversed(range(mesh.shape["dom"].bit_length() - 1)))
    names = traj_axes + dom_axes
    bit_mesh = Mesh(mesh.devices.reshape((2,) * len(names)), names)
    rows = P(traj_axes, dom_axes, None)
    in_specs = (rows,) * 4 + (P(),) * 4 + (P(dom_axes),) * 4
    out_specs = (rows,) * 3 + (P(None, dom_axes, None),)

    def body(*arrays):
        return per_device(traj_axes, dom_axes, *arrays)

    return jax.shard_map(
        body, mesh=bit_mesh, in_specs=in_specs, out_specs=out_specs, check_vma=False
    )
```

```python
import functools

import jax
import jax.numpy as jnp
from jax import lax
from jax.experimental import pallas as pl
from jax.experimental.pallas import tpu as pltpu
from jax.sharding import Mesh, PartitionSpec as P


LANES = 128
ROOM = 24 << 20
BF16 = jnp.bfloat16
F32 = jnp.float32
VMEM = pl.BlockSpec(memory_space=pltpu.VMEM)
SMEM = pl.BlockSpec(memory_space=pltpu.SMEM)


def dot(former, latter):
    return jnp.dot(former, latter, preferred_element_type=F32)


def dot_rows(former, latter):
    return lax.dot_general(former, latter, (((0,), (0,)), ((), ())), preferred_element_type=F32)


def dot_cols(former, latter):
    return lax.dot_general(former, latter, (((1,), (1,)), ((), ())), preferred_element_type=F32)


def near(array):
    return pltpu.with_memory_space_constraint(array, pltpu.VMEM)


def far(array):
    return pltpu.with_memory_space_constraint(array, pltpu.HBM)


def call(body, outs, ins, kept=True, scratch=()):
    fresh = pltpu.VMEM if kept else jax.ShapeDtypeStruct
    return pl.pallas_call(
        body,
        out_shape=[fresh(shape, kind) for shape, kind in outs],
        in_specs=ins,
        out_specs=[VMEM] * len(outs),
        scratch_shapes=scratch,
        compiler_params=pltpu.CompilerParams(vmem_limit_bytes=ROOM),
    )


def swap(array, axis):
    return lax.ppermute(array, axis, [(0, 1), (1, 0)])


def down_rows(row, count):
    return jnp.transpose(jnp.broadcast_to(row, (LANES, count)))


def onehot_cols(index_cols, first, blocks):
    lane = lax.broadcasted_iota(jnp.int32, index_cols.shape, 1)
    parts = [
        jnp.where(index_cols == lane + (first + LANES * block), 1.0, 0.0).astype(BF16)
        for block in range(blocks)
    ]
    return jnp.concatenate(parts, axis=1)


def onehot_rows(index_row, first, rows):
    node = lax.broadcasted_iota(jnp.int32, (rows, index_row.shape[1]), 0) + first
    return jnp.where(node == index_row, 1.0, 0.0).astype(BF16)


def receiver_row(recv_block, recv_node):
    edges = recv_node.shape[1]
    return jnp.concatenate(
        [
            recv_node[:, LANES * block : LANES * (block + 1)] + recv_block[block] * LANES
            for block in range(edges // LANES)
        ],
        axis=1,
    )


def pick_body(send_blocks, node_lat, *lent):
    for section, out in enumerate(lent):
        out[...] = node_lat[pl.ds(pl.multiple_of(send_blocks[section] * LANES, LANES), LANES), :]


def early_body(
    rounds, recv_block, send_blocks, edge_src, recv_node, node_lat, edge_lat, grad_edge, grad_agg, weight_edge,
    weight_recv, blocks_out, sender_out, receiver_out, edge_out, recv_out, send_out, hot_out,
    preact_out, grad_msg_out,
):
    nodes = node_lat.shape[0]
    edges = edge_lat.shape[0]
    row = receiver_row(recv_block, recv_node[...])
    receiver_out[...] = row
    blocks_out[...] = send_blocks[...]
    sender_out[...] = edge_src[...]
    edge_out[...] = edge_lat[...]
    receiver = down_rows(row, edges)
    sender = down_rows(edge_src[...], edges)
    hot_recv = onehot_cols(receiver, 0, nodes // LANES)
    recv_rows = dot(hot_recv, node_lat[...]).astype(BF16)
    recv_out[...] = recv_rows
    send_out[...] = dot(onehot_cols(sender, 0, nodes // LANES), node_lat[...]).astype(BF16)
    hot_out[...] = onehot_cols(sender, nodes, rounds)
    preact_out[...] = dot(edge_lat[...], weight_edge[...]) + dot(recv_rows, weight_recv[...])
    grad_msg = grad_edge[...].astype(F32) + dot(hot_recv, grad_agg[...])
    grad_msg_out[...] = grad_msg - jnp.mean(grad_msg, axis=1, keepdims=True)


def place_of(split, dom_axes):
    domain = 0
    for axis in dom_axes:
        domain = domain * 2 + lax.axis_index(axis)
    return lax.axis_index(split[0]) if split else 0, domain


def store_rows(target, at, blocks):
    run = []
    for block in blocks:
        run.append(block)
        rows = sum(part.shape[0] for part in run)
        if rows % 16 == 0:
            whole = run[0] if len(run) == 1 else jnp.concatenate(run, axis=0)
            target[at : at + rows, :] = whole.astype(target.dtype)
            at += rows
            run = []


def give_rows(domains, where, sums, give_out, at=0):
    _, own = where()
    store_rows(give_out, at, [sums[own ^ (domain | 1)] for domain in domains])


def main_body(
    rounds, domains, where, send_own, hot, preact_own, grad_msg, weight_send, weight_out, *refs
):
    borrowed = refs[:rounds]
    send_out, grad_preact_out, message_out, sums_out, give_out, table = refs[rounds:]
    for section in range(rounds):
        table[LANES * section : LANES * (section + 1), :] = borrowed[section][...]
    send = (send_own[...].astype(F32) + dot(hot[...], table[...])).astype(BF16)
    send_out[...] = send
    preact = preact_own[...] + dot(send, weight_send[...])
    sigmoid = jax.nn.sigmoid(preact)
    hidden = (preact * sigmoid).astype(BF16)
    slope = sigmoid * (1.0 + preact * (1.0 - sigmoid))
    projected = dot(hidden, weight_out[...])
    centered = projected - jnp.mean(projected, axis=1, keepdims=True)
    inv_std = lax.rsqrt(jnp.mean(centered * centered, axis=1, keepdims=True) + 1e-05)
    normed = centered * inv_std
    message_out[...] = normed.astype(BF16)
    grad = grad_msg[...]
    grad_proj = inv_std * (grad - normed * jnp.mean(grad * normed, axis=1, keepdims=True))
    grad_proj = grad_proj.astype(BF16)
    grad_preact_out[...] = (dot_cols(grad_proj, weight_out[...]) * slope).astype(BF16)
    sums_out[...] = dot_rows(hidden, grad_proj).reshape(sums_out.shape)
    give_rows(domains, where, sums_out, give_out)


def grads_body(domains, where, *refs):
    *sums_outs, give_out = refs[-(len(refs) // 3) - 1 :]
    for which, sums_out in enumerate(sums_outs):
        former, latter = refs[2 * which : 2 * which + 2]
        sums_out[...] = dot_rows(former[...], latter[...]).reshape(sums_out.shape)
        rows = give_out.shape[0] // len(sums_outs)
        give_rows(domains, where, sums_out, give_out, which * rows)


def chip_body(plan, parts, where, places, *refs):
    keep_out, give_out = refs[-2:]
    sums, gots = refs[: len(places)], refs[len(places) : -2]
    count = len(sums) // parts
    part, own = where()
    half = len(plan) // 2

    def add(which, index, domain):
        share = sums[which].shape[1]
        holder, first = places[which]
        first += index * share
        start = first // 16 * 16
        got = gots[holder][start : start + max(share, 16), :].astype(F32)
        return sums[which][own ^ domain] + got[first - start : first - start + share]

    def write(this):
        for target, pieces in ((give_out, plan[half:]), (keep_out, plan[:half])):
            store_rows(
                target,
                0,
                [
                    add((this ^ flip) * count + which, index, domain)
                    for flip, index, domain in pieces
                    for which in range(count)
                ],
            )

    if parts == 1:
        write(0)
    else:
        for this in range(parts):
            pl.when(part == this)(functools.partial(write, this))


def sums_body(edge_src, receiver, grad_preact, own_out, recv_out, *back_out):
    nodes = own_out.shape[0]
    rounds = len(back_out)
    rows = grad_preact[...]
    slot_sums = dot(onehot_rows(edge_src[...], 0, nodes + rounds * LANES), rows)
    own_out[...] = slot_sums[:nodes]
    for section in range(rounds):
        first = nodes + LANES * section
        back_out[section][...] = slot_sums[first : first + LANES].astype(BF16)
    recv_out[...] = dot(onehot_rows(receiver[...], 0, nodes), rows)


def split_body(keep, got, keep_out, give_out):
    half = keep.shape[0] // 2
    for target, first in ((give_out, half), (keep_out, 0)):
        rows = slice(first, first + half)
        target[...] = (keep[rows, :] + got[rows, :].astype(F32)).astype(target.dtype)


def round_body(keep, got, out):
    out[...] = (keep[...] + got[...].astype(F32)).astype(BF16)


def finish_body(where, *refs):
    *parts, out = refs
    own, _ = where()
    if len(parts) == 4:
        whole, split, whole_got, split_got = parts
        take = split.shape[0]
        total = whole[...].astype(F32) + whole_got[...].astype(F32)
        for half in range(2):
            out[2 * half * take : (2 * half + 1) * take, :] = total[half * take : (half + 1) * take]
        for flip, part in enumerate((split, split_got)):
            first = pl.multiple_of((2 * (own ^ flip) + 1) * take, take)
            out[pl.ds(first, take), :] = part[...].astype(F32)
    else:
        take = parts[0].shape[0]
        for flip, part in enumerate(parts):
            first = pl.multiple_of((own ^ flip) * take, take)
            out[pl.ds(first, take), :] = part[...].astype(F32)


def edge_body(receiver, grad_preact, message, grad_edge, weight_edge, agg_out, edge_out):
    agg_out[...] = dot(onehot_rows(receiver[...], 0, agg_out.shape[0]), message[...]).astype(BF16)
    edge_out[...] = (
        grad_edge[...].astype(F32) + dot_cols(grad_preact[...], weight_edge[...])
    ).astype(BF16)


def dot_cols_split(former, latter):
    high = former.astype(BF16)
    low = (former - high.astype(F32)).astype(BF16)
    return dot_cols(high, latter) + dot_cols(low, latter)


def node_body(send_blocks, own_sums, recv_sums, weight_send, weight_recv, *refs):
    returned, out, total = refs[:-2], refs[-2], refs[-1]
    for first in range(0, out.shape[0], LANES):
        rows = slice(first, first + LANES)
        summed = own_sums[rows, :]
        for section, block in enumerate(returned):
            mine = send_blocks[:, section : section + 1] == first // LANES
            summed = summed + jnp.where(mine, block[...].astype(F32), 0.0)
        total[rows, :] = summed
    out[...] = (
        dot_cols_split(total[...], weight_send[...])
        + dot_cols_split(recv_sums[...], weight_recv[...])
    ).astype(BF16)


def layout(share, parts, tops):
    colours = 2 if parts == 2 and tops and share >= 16 else 1
    orders = [(["part"] if parts == 2 else []) + list(range(1, tops + 1))]
    if colours == 2:
        orders.insert(0, list(range(1, tops + 1)))
    domains = [index << 1 for index in range(2**tops)]
    plans = []
    for order in orders:
        pieces = []
        for index in range(2 ** len(order)):
            domain, flip = 0, 0
            for level, bit in enumerate(order):
                on = index >> (len(order) - 1 - level) & 1
                if bit == "part":
                    flip = on
                else:
                    domain |= on << bit
            pieces.append((flip, domain >> 1, domain))
        plans.append(pieces)
    return plans, orders, domains


def per_device(
    traj_axes, dom_axes, node_lat, edge_lat, grad_edge, grad_agg, weight_edge, weight_send,
    weight_recv, weight_out, edge_src, edge_recv_block, edge_recv_node, send_blocks,
):
    node_lat, edge_lat, grad_edge, grad_agg = node_lat[0], edge_lat[0], grad_edge[0], grad_agg[0]
    nodes, features = node_lat.shape
    edges = edge_lat.shape[0]
    rounds = send_blocks.shape[0]
    edge_src = edge_src.reshape(1, edges)
    recv_node = edge_recv_node.reshape(1, edges)
    bits = dom_axes[::-1]
    share = features // 2 ** len(bits)
    split = traj_axes[:1] if 2 * share >= 16 else ()
    plans, orders, domains = layout(share, 1 + len(split), len(bits) - 1)
    colours = len(orders)
    half = 2 * features
    wide = ((edges, features), BF16)
    wide_sum = ((edges, features), F32)
    node_sum = ((nodes, features), F32)
    block = ((LANES, features), BF16)
    where = functools.partial(place_of, split, dom_axes)

    lent = call(pick_body, [block] * rounds, [SMEM, VMEM])(
        far(send_blocks), far(node_lat)
    )
    borrowed = [swap(lent[section], bits[section]) for section in range(rounds)]
    blocks, sender, receiver, edge_rows, recv_rows, send_own, hot, preact_own, grad_msg = call(
        functools.partial(early_body, rounds),
        [((1, rounds), jnp.int32)] + [((1, edges), jnp.int32)] * 2 + [wide, wide, wide, ((edges, rounds * LANES), BF16), wide_sum, wide_sum],
        [SMEM] + [VMEM] * 9,
    )(
        *map(far, (edge_recv_block, send_blocks.reshape(1, rounds), edge_src, recv_node)),
        *map(far, (node_lat, edge_lat)),
        *map(far, (grad_edge, grad_agg, weight_edge, weight_recv)),
    )
    sum_rows = [
        ((2 ** len(bits), share, features), F32), ((share * len(domains), features), BF16)
    ]
    sums, gives = [None] * 4, [None] * 4
    send_rows, grad_preact, message, sums[3], gives[3] = call(
        functools.partial(main_body, rounds, domains, where),
        [wide] * 3 + sum_rows,
        [VMEM] * (6 + rounds),
        scratch=[pltpu.VMEM((rounds * LANES, features), BF16)],
    )(
        send_own, hot, preact_own, grad_msg, near(weight_send), near(weight_out),
        *map(near, borrowed),
    )
    factors = {0: (edge_rows, grad_preact), 1: (send_rows, grad_preact), 2: (recv_rows, grad_preact)}
    gave = {(3,): gives[3]}
    for group in ((1,), (0, 2)):
        shape, (give_shape, kind) = sum_rows
        *made, gave[group] = call(
            functools.partial(grads_body, domains, where),
            [shape] * len(group) + [((give_shape[0] * len(group), features), kind)],
            [VMEM] * (2 * len(group)),
        )(*sum((factors[which] for which in group), ()))
        for which, array in zip(group, made):
            sums[which] = array
    came = {group: near(swap(give, bits[0])) for group, give in gave.items()}
    flows, places = [], []
    for colour in range(colours):
        used = range(4)[colour::colours]
        groups = [group for group in came if set(group) & set(used)]
        rows = share * len(domains)
        places.append(
            [
                (holder, group.index(which) * rows)
                for which in used
                for holder, group in enumerate(groups)
                if which in group
            ]
        )
        flows.append([sums[which] for which in used] + [came[group] for group in groups])
    rows = half // colours

    own_sums, recv_sums, *back = call(
        sums_body, [node_sum, node_sum] + [block] * rounds, [VMEM] * 3
    )(sender, receiver, grad_preact)
    returned = [swap(back[section], bits[section]) for section in range(rounds)]

    def halves(rows):
        return [((rows, features), F32), ((rows, features), BF16)]

    depths = [len(order) for order in orders]
    for level in range(max(depths)):
        rows //= 2
        for colour, order in enumerate(orders):
            if level >= depths[colour]:
                continue
            if level:
                fold = call(split_body, halves(rows), [VMEM] * 2)
            else:
                parts = 2 if "part" in order else 1
                body = functools.partial(chip_body, plans[colour], parts, where, places[colour])
                fold = call(body, halves(rows), [VMEM] * len(flows[colour]))
            keep, give = fold(*flows[colour])
            axis = split[0] if order[level] == "part" else bits[order[level]]
            flows[colour] = (keep, near(swap(give, axis)))
    totals = []
    for flow in flows:
        sized = [((flow[0].shape[0], features), BF16)]
        (total,) = call(round_body, sized, [VMEM] * 2)(*flow)
        for axis in traj_axes[len(split) :]:
            (total,) = call(round_body, sized, [VMEM] * 2)(total, near(swap(total, axis)))
        totals.append(total)
    totals += [near(swap(total, axis)) for axis in split for total in totals]
    (weight_grads,) = call(
        functools.partial(finish_body, where),
        [((4 * share, features), F32)],
        [VMEM] * len(totals),
        kept=False,
    )(*totals)
    agg, grad_edges = call(
        edge_body, [((nodes, features), BF16), wide], [VMEM] * 5, kept=False
    )(receiver, grad_preact, message, near(grad_edge), near(weight_edge))
    (grad_nodes,) = call(
        node_body,
        [((nodes, features), BF16)],
        [VMEM] * (5 + rounds),
        kept=False,
        scratch=[pltpu.VMEM((nodes, features), F32)],
    )(
        blocks, own_sums, recv_sums, near(weight_send), near(weight_recv),
        *map(near, returned),
    )
    return agg[None], grad_edges[None], grad_nodes[None], weight_grads.reshape(4, share, features)


def solution(mesh):
    traj_axes = tuple(f"t{bit}" for bit in reversed(range(mesh.shape["traj"].bit_length() - 1)))
    dom_axes = tuple(f"d{bit}" for bit in reversed(range(mesh.shape["dom"].bit_length() - 1)))
    names = traj_axes + dom_axes
    bit_mesh = Mesh(mesh.devices.reshape((2,) * len(names)), names)
    rows = P(traj_axes, dom_axes, None)
    in_specs = (rows,) * 4 + (P(),) * 4 + (P(dom_axes),) * 4
    out_specs = (rows,) * 3 + (P(None, dom_axes, None),)

    def body(*arrays):
        return per_device(traj_axes, dom_axes, *arrays)

    return jax.shard_map(
        body, mesh=bit_mesh, in_specs=in_specs, out_specs=out_specs, check_vma=False
    )
```

```python
import functools

import jax
import jax.numpy as jnp
from jax import lax
from jax.experimental import pallas as pl
from jax.experimental.pallas import tpu as pltpu
from jax.sharding import Mesh, PartitionSpec as P


LANES = 128
ROOM = 24 << 20
BF16 = jnp.bfloat16
F32 = jnp.float32
VMEM = pl.BlockSpec(memory_space=pltpu.VMEM)
SMEM = pl.BlockSpec(memory_space=pltpu.SMEM)


def dot(former, latter):
    return jnp.dot(former, latter, preferred_element_type=F32)


def dot_rows(former, latter):
    return lax.dot_general(former, latter, (((0,), (0,)), ((), ())), preferred_element_type=F32)


def dot_cols(former, latter):
    return lax.dot_general(former, latter, (((1,), (1,)), ((), ())), preferred_element_type=F32)


def near(array):
    return pltpu.with_memory_space_constraint(array, pltpu.VMEM)


def far(array):
    return pltpu.with_memory_space_constraint(array, pltpu.HBM)


def call(body, outs, ins, kept=True, scratch=()):
    fresh = pltpu.VMEM if kept else jax.ShapeDtypeStruct
    return pl.pallas_call(
        body,
        out_shape=[fresh(shape, kind) for shape, kind in outs],
        in_specs=ins,
        out_specs=[VMEM] * len(outs),
        scratch_shapes=scratch,
        compiler_params=pltpu.CompilerParams(vmem_limit_bytes=ROOM),
    )


def swap(array, axis):
    return lax.ppermute(array, axis, [(0, 1), (1, 0)])


def down_rows(row, count):
    return jnp.transpose(jnp.broadcast_to(row, (LANES, count)))


def onehot_cols(index_cols, first, blocks):
    lane = lax.broadcasted_iota(jnp.int32, index_cols.shape, 1)
    parts = [
        jnp.where(index_cols == lane + (first + LANES * block), 1.0, 0.0).astype(BF16)
        for block in range(blocks)
    ]
    return jnp.concatenate(parts, axis=1)


def onehot_rows(index_row, first, rows):
    node = lax.broadcasted_iota(jnp.int32, (rows, index_row.shape[1]), 0) + first
    return jnp.where(node == index_row, 1.0, 0.0).astype(BF16)


def receiver_row(recv_block, recv_node):
    edges = recv_node.shape[1]
    return jnp.concatenate(
        [
            recv_node[:, LANES * block : LANES * (block + 1)] + recv_block[block] * LANES
            for block in range(edges // LANES)
        ],
        axis=1,
    )


def pick_body(send_blocks, node_lat, *lent):
    for section, out in enumerate(lent):
        out[...] = node_lat[pl.ds(pl.multiple_of(send_blocks[section] * LANES, LANES), LANES), :]


def early_body(
    rounds, recv_block, send_blocks, edge_src, recv_node, node_lat, edge_lat, grad_edge, grad_agg, weight_edge,
    weight_recv, blocks_out, sender_out, receiver_out, edge_out, recv_out, send_out, hot_out,
    preact_out, grad_msg_out,
):
    nodes = node_lat.shape[0]
    edges = edge_lat.shape[0]
    row = receiver_row(recv_block, recv_node[...])
    receiver_out[...] = row
    blocks_out[...] = send_blocks[...]
    sender_out[...] = edge_src[...]
    edge_out[...] = edge_lat[...]
    receiver = down_rows(row, edges)
    sender = down_rows(edge_src[...], edges)
    hot_recv = onehot_cols(receiver, 0, nodes // LANES)
    recv_rows = dot(hot_recv, node_lat[...]).astype(BF16)
    recv_out[...] = recv_rows
    send_out[...] = dot(onehot_cols(sender, 0, nodes // LANES), node_lat[...]).astype(BF16)
    hot_out[...] = onehot_cols(sender, nodes, rounds)
    preact_out[...] = dot(edge_lat[...], weight_edge[...]) + dot(recv_rows, weight_recv[...])
    grad_msg = grad_edge[...].astype(F32) + dot(hot_recv, grad_agg[...])
    grad_msg_out[...] = grad_msg - jnp.mean(grad_msg, axis=1, keepdims=True)


def place_of(split, dom_axes):
    domain = 0
    for axis in dom_axes:
        domain = domain * 2 + lax.axis_index(axis)
    return lax.axis_index(split[0]) if split else 0, domain


def store_rows(target, at, blocks):
    run = []
    for block in blocks:
        run.append(block)
        rows = sum(part.shape[0] for part in run)
        if rows % 16 == 0:
            whole = run[0] if len(run) == 1 else jnp.concatenate(run, axis=0)
            target[at : at + rows, :] = whole.astype(target.dtype)
            at += rows
            run = []


def give_rows(domains, where, sums, give_out, at=0):
    _, own = where()
    store_rows(give_out, at, [sums[own ^ (domain | 1)] for domain in domains])


def main_body(
    rounds, domains, where, send_own, hot, preact_own, grad_msg, weight_send, weight_out, *refs
):
    borrowed = refs[:rounds]
    send_out, grad_preact_out, message_out, sums_out, give_out, table = refs[rounds:]
    for section in range(rounds):
        table[LANES * section : LANES * (section + 1), :] = borrowed[section][...]
    send = (send_own[...].astype(F32) + dot(hot[...], table[...])).astype(BF16)
    send_out[...] = send
    preact = preact_own[...] + dot(send, weight_send[...])
    sigmoid = jax.nn.sigmoid(preact)
    product = preact * sigmoid
    hidden = product.astype(BF16)
    slope = sigmoid + product * (1.0 - sigmoid)
    projected = dot(hidden, weight_out[...])
    centered = projected - jnp.mean(projected, axis=1, keepdims=True)
    inv_std = lax.rsqrt(jnp.mean(centered * centered, axis=1, keepdims=True) + 1e-05)
    normed = centered * inv_std
    message_out[...] = normed.astype(BF16)
    grad = grad_msg[...]
    grad_proj = inv_std * (grad - normed * jnp.mean(grad * normed, axis=1, keepdims=True))
    grad_proj = grad_proj.astype(BF16)
    grad_preact_out[...] = (dot_cols(grad_proj, weight_out[...]) * slope).astype(BF16)
    sums_out[...] = dot_rows(hidden, grad_proj).reshape(sums_out.shape)
    give_rows(domains, where, sums_out, give_out)


def grads_body(domains, where, *refs):
    *sums_outs, give_out = refs[-(len(refs) // 3) - 1 :]
    for which, sums_out in enumerate(sums_outs):
        former, latter = refs[2 * which : 2 * which + 2]
        sums_out[...] = dot_rows(former[...], latter[...]).reshape(sums_out.shape)
        rows = give_out.shape[0] // len(sums_outs)
        give_rows(domains, where, sums_out, give_out, which * rows)


def chip_body(plan, parts, where, places, *refs):
    keep_out, give_out = refs[-2:]
    sums, gots = refs[: len(places)], refs[len(places) : -2]
    count = len(sums) // parts
    part, own = where()
    half = len(plan) // 2

    def add(which, index, domain):
        share = sums[which].shape[1]
        holder, first = places[which]
        first += index * share
        start = first // 16 * 16
        got = gots[holder][start : start + max(share, 16), :].astype(F32)
        return sums[which][own ^ domain] + got[first - start : first - start + share]

    def write(this):
        for target, pieces in ((give_out, plan[half:]), (keep_out, plan[:half])):
            store_rows(
                target,
                0,
                [
                    add((this ^ flip) * count + which, index, domain)
                    for flip, index, domain in pieces
                    for which in range(count)
                ],
            )

    if parts == 1:
        write(0)
    else:
        for this in range(parts):
            pl.when(part == this)(functools.partial(write, this))


def sums_body(edge_src, receiver, grad_preact, own_out, recv_out, *back_out):
    nodes = own_out.shape[0]
    rounds = len(back_out)
    rows = grad_preact[...]
    slot_sums = dot(onehot_rows(edge_src[...], 0, nodes + rounds * LANES), rows)
    own_out[...] = slot_sums[:nodes]
    for section in range(rounds):
        first = nodes + LANES * section
        back_out[section][...] = slot_sums[first : first + LANES].astype(BF16)
    recv_out[...] = dot(onehot_rows(receiver[...], 0, nodes), rows)


def split_body(keep, got, keep_out, give_out):
    half = keep.shape[0] // 2
    for target, first in ((give_out, half), (keep_out, 0)):
        rows = slice(first, first + half)
        target[...] = (keep[rows, :] + got[rows, :].astype(F32)).astype(target.dtype)


def round_body(keep, got, out):
    out[...] = (keep[...] + got[...].astype(F32)).astype(BF16)


def finish_body(where, *refs):
    *parts, out = refs
    own, _ = where()
    if len(parts) == 4:
        whole, split, whole_got, split_got = parts
        take = split.shape[0]
        total = whole[...].astype(F32) + whole_got[...].astype(F32)
        for half in range(2):
            out[2 * half * take : (2 * half + 1) * take, :] = total[half * take : (half + 1) * take]
        for flip, part in enumerate((split, split_got)):
            first = pl.multiple_of((2 * (own ^ flip) + 1) * take, take)
            out[pl.ds(first, take), :] = part[...].astype(F32)
    else:
        take = parts[0].shape[0]
        for flip, part in enumerate(parts):
            first = pl.multiple_of((own ^ flip) * take, take)
            out[pl.ds(first, take), :] = part[...].astype(F32)


def edge_body(receiver, grad_preact, message, grad_edge, weight_edge, agg_out, edge_out):
    agg_out[...] = dot(onehot_rows(receiver[...], 0, agg_out.shape[0]), message[...]).astype(BF16)
    edge_out[...] = (
        grad_edge[...].astype(F32) + dot_cols(grad_preact[...], weight_edge[...])
    ).astype(BF16)


def dot_cols_split(former, latter):
    high = former.astype(BF16)
    low = (former - high.astype(F32)).astype(BF16)
    return dot_cols(high, latter) + dot_cols(low, latter)


def node_body(send_blocks, own_sums, recv_sums, weight_send, weight_recv, *refs):
    returned, out, total = refs[:-2], refs[-2], refs[-1]
    for first in range(0, out.shape[0], LANES):
        rows = slice(first, first + LANES)
        summed = own_sums[rows, :]
        for section, block in enumerate(returned):
            mine = send_blocks[:, section : section + 1] == first // LANES
            summed = summed + jnp.where(mine, block[...].astype(F32), 0.0)
        total[rows, :] = summed
    out[...] = (
        dot_cols_split(total[...], weight_send[...])
        + dot_cols_split(recv_sums[...], weight_recv[...])
    ).astype(BF16)


def layout(share, parts, tops):
    colours = 2 if parts == 2 and tops and share >= 16 else 1
    orders = [(["part"] if parts == 2 else []) + list(range(1, tops + 1))]
    if colours == 2:
        orders.insert(0, list(range(1, tops + 1)))
    domains = [index << 1 for index in range(2**tops)]
    plans = []
    for order in orders:
        pieces = []
        for index in range(2 ** len(order)):
            domain, flip = 0, 0
            for level, bit in enumerate(order):
                on = index >> (len(order) - 1 - level) & 1
                if bit == "part":
                    flip = on
                else:
                    domain |= on << bit
            pieces.append((flip, domain >> 1, domain))
        plans.append(pieces)
    return plans, orders, domains


def per_device(
    traj_axes, dom_axes, node_lat, edge_lat, grad_edge, grad_agg, weight_edge, weight_send,
    weight_recv, weight_out, edge_src, edge_recv_block, edge_recv_node, send_blocks,
):
    node_lat, edge_lat, grad_edge, grad_agg = node_lat[0], edge_lat[0], grad_edge[0], grad_agg[0]
    nodes, features = node_lat.shape
    edges = edge_lat.shape[0]
    rounds = send_blocks.shape[0]
    edge_src = edge_src.reshape(1, edges)
    recv_node = edge_recv_node.reshape(1, edges)
    bits = dom_axes[::-1]
    share = features // 2 ** len(bits)
    split = traj_axes[:1] if 2 * share >= 16 else ()
    plans, orders, domains = layout(share, 1 + len(split), len(bits) - 1)
    colours = len(orders)
    half = 2 * features
    wide = ((edges, features), BF16)
    wide_sum = ((edges, features), F32)
    node_sum = ((nodes, features), F32)
    block = ((LANES, features), BF16)
    where = functools.partial(place_of, split, dom_axes)

    lent = call(pick_body, [block] * rounds, [SMEM, VMEM])(
        far(send_blocks), far(node_lat)
    )
    borrowed = [swap(lent[section], bits[section]) for section in range(rounds)]
    blocks, sender, receiver, edge_rows, recv_rows, send_own, hot, preact_own, grad_msg = call(
        functools.partial(early_body, rounds),
        [((1, rounds), jnp.int32)] + [((1, edges), jnp.int32)] * 2 + [wide, wide, wide, ((edges, rounds * LANES), BF16), wide_sum, wide_sum],
        [SMEM] + [VMEM] * 9,
    )(
        *map(far, (edge_recv_block, send_blocks.reshape(1, rounds), edge_src, recv_node)),
        *map(far, (node_lat, edge_lat)),
        *map(far, (grad_edge, grad_agg, weight_edge, weight_recv)),
    )
    sum_rows = [
        ((2 ** len(bits), share, features), F32), ((share * len(domains), features), BF16)
    ]
    sums, gives = [None] * 4, [None] * 4
    send_rows, grad_preact, message, sums[3], gives[3] = call(
        functools.partial(main_body, rounds, domains, where),
        [wide] * 3 + sum_rows,
        [VMEM] * (6 + rounds),
        scratch=[pltpu.VMEM((rounds * LANES, features), BF16)],
    )(
        send_own, hot, preact_own, grad_msg, near(weight_send), near(weight_out),
        *map(near, borrowed),
    )
    factors = {0: (edge_rows, grad_preact), 1: (send_rows, grad_preact), 2: (recv_rows, grad_preact)}
    gave = {(3,): gives[3]}
    for group in ((1,), (0, 2)):
        shape, (give_shape, kind) = sum_rows
        *made, gave[group] = call(
            functools.partial(grads_body, domains, where),
            [shape] * len(group) + [((give_shape[0] * len(group), features), kind)],
            [VMEM] * (2 * len(group)),
        )(*sum((factors[which] for which in group), ()))
        for which, array in zip(group, made):
            sums[which] = array
    came = {group: near(swap(give, bits[0])) for group, give in gave.items()}
    flows, places = [], []
    for colour in range(colours):
        used = range(4)[colour::colours]
        groups = [group for group in came if set(group) & set(used)]
        rows = share * len(domains)
        places.append(
            [
                (holder, group.index(which) * rows)
                for which in used
                for holder, group in enumerate(groups)
                if which in group
            ]
        )
        flows.append([sums[which] for which in used] + [came[group] for group in groups])
    rows = half // colours

    own_sums, recv_sums, *back = call(
        sums_body, [node_sum, node_sum] + [block] * rounds, [VMEM] * 3
    )(sender, receiver, grad_preact)
    returned = [swap(back[section], bits[section]) for section in range(rounds)]

    def halves(rows):
        return [((rows, features), F32), ((rows, features), BF16)]

    depths = [len(order) for order in orders]
    for level in range(max(depths)):
        rows //= 2
        for colour, order in enumerate(orders):
            if level >= depths[colour]:
                continue
            if level:
                fold = call(split_body, halves(rows), [VMEM] * 2)
            else:
                parts = 2 if "part" in order else 1
                body = functools.partial(chip_body, plans[colour], parts, where, places[colour])
                fold = call(body, halves(rows), [VMEM] * len(flows[colour]))
            keep, give = fold(*flows[colour])
            axis = split[0] if order[level] == "part" else bits[order[level]]
            flows[colour] = (keep, near(swap(give, axis)))
    totals = []
    for flow in flows:
        sized = [((flow[0].shape[0], features), BF16)]
        (total,) = call(round_body, sized, [VMEM] * 2)(*flow)
        for axis in traj_axes[len(split) :]:
            (total,) = call(round_body, sized, [VMEM] * 2)(total, near(swap(total, axis)))
        totals.append(total)
    totals += [near(swap(total, axis)) for axis in split for total in totals]
    (weight_grads,) = call(
        functools.partial(finish_body, where),
        [((4 * share, features), F32)],
        [VMEM] * len(totals),
        kept=False,
    )(*totals)
    agg, grad_edges = call(
        edge_body, [((nodes, features), BF16), wide], [VMEM] * 5, kept=False
    )(receiver, grad_preact, message, near(grad_edge), near(weight_edge))
    (grad_nodes,) = call(
        node_body,
        [((nodes, features), BF16)],
        [VMEM] * (5 + rounds),
        kept=False,
        scratch=[pltpu.VMEM((nodes, features), F32)],
    )(
        blocks, own_sums, recv_sums, near(weight_send), near(weight_recv),
        *map(near, returned),
    )
    return agg[None], grad_edges[None], grad_nodes[None], weight_grads.reshape(4, share, features)


def solution(mesh):
    traj_axes = tuple(f"t{bit}" for bit in reversed(range(mesh.shape["traj"].bit_length() - 1)))
    dom_axes = tuple(f"d{bit}" for bit in reversed(range(mesh.shape["dom"].bit_length() - 1)))
    names = traj_axes + dom_axes
    bit_mesh = Mesh(mesh.devices.reshape((2,) * len(names)), names)
    rows = P(traj_axes, dom_axes, None)
    in_specs = (rows,) * 4 + (P(),) * 4 + (P(dom_axes),) * 4
    out_specs = (rows,) * 3 + (P(None, dom_axes, None),)

    def body(*arrays):
        return per_device(traj_axes, dom_axes, *arrays)

    return jax.shard_map(
        body, mesh=bit_mesh, in_specs=in_specs, out_specs=out_specs, check_vma=False
    )
```
